32 devices in a mesh: dp: 16 (over z, x, core), mp: 2 (over y).
Axes of the slice: x: 2, y: 2, z: 4, core: 2. Of those that a mesh axis runs over, the one named last changes fastest.
Arguments:
- attn_out: bfloat16 [3072, 1536], P('dp', 'mp'), may hold values from -6 to 6
- residual: bfloat16 [3072, 1536], P('dp', 'mp')
- out_proj: bfloat16 [1536, 1536], P(None, 'mp'), may hold values from -0.15625 to 0.15625
- gain_attn: float32 [1536], P('mp'), may hold values from 0.25 to 1.75
- routes: int32 [3072, 8], P('dp'), may hold values from 0 to 47, all different within a row; in each aligned block of 192 rows (0 to 191, 192 to 383, ...) at most 40 rows name the same one
- gate_weights: float32 [3072, 8], P('dp'), may hold values from 0.05 to 0.5
- gate_up: bfloat16 [48, 1536, 2, 512], P('dp', 'mp')
- down_proj: bfloat16 [48, 512, 1536], P('dp', None, 'mp')
- gain_moe: float32 [1536], P('mp'), may hold values from 0.25 to 1.75
- kv_proj: bfloat16 [1536, 1024], P(None, 'mp'), may hold values from -0.15625 to 0.15625
- prompt_lens: int32 [16], replicated, may hold values from 1 to 760, 3040 in all
- decode_pos: int32 [32], replicated, may hold values from 0 to 1023
- page_table: int32 [48, 8], replicated, may hold values from 0 to 383, as said below
- kv_cache: bfloat16 [384, 128, 1024], P('dp', None, 'mp'), may hold values from -6 to 6
Outputs:
- layer_out: bfloat16 [3072, 1536], P('dp', 'mp')
- cache_out: bfloat16 [384, 128, 1024], P('dp', None, 'mp')
The draws below stay inside these ranges and needn't reach their ends.
Inputs may be any that keep to these rules, and one draw needn't show every extreme that they name: In each aligned block of 192 rows (the rows of one index of dp), no slot is named by more than 40 routes, a bound that some block reaches. Slot s is held by dp index s // 3. `page_table`: all entries are distinct; page n lies on dp index n // 24. `prompt_lens`: they sum to the prefill rows of all dp indices.
All inputs are finite; a program needn't handle non-finite values.
Results may differ from the reference program's by a relative error of at most 0.0095.
Values may be sent and summed in bfloat16 or wider, within the bound.
No kernel may reach another device: no remote copies, remote signals or barrier semaphores. Data moves between devices by JAX's collectives and lax.ppermute only.
A program may use at most 128 MiB of HBM per device.

```python
import math
import jax
import jax.numpy as jnp
import numpy as np
from jax import lax

D = 1536
E = 40
FF = 512
TOP = 8
KVH = 8
HD = 64
PAGE = 128
PAGES_SEQ = 8
DEC_DEV = 2
ROWS_DEV = 192
PRE_DEV = 190
TOKENS = 3072
PROMPTS = 16
DECODES = 32
SEQ_ALL = 48
SLOTS = 48
CAP = 40
TOTAL_PAGES = 384
MAXLEN = 1024
LONGEST = 760
KV2 = 1024
N_DP = 16
N_MP = 2


def expert_owner(key):
    inner = jax.random.fold_in(key, 101)
    first_key, second_key = jax.random.split(inner)
    extra = jax.random.randint(first_key, (SLOTS - E,), 0, E, dtype=jnp.int32)
    base = jnp.concatenate([jnp.arange(E, dtype=jnp.int32), extra])
    order = jax.random.permutation(second_key, SLOTS)
    return base[order]


def draw_gate_up(key, part):
    owner = expert_owner(key)
    inner = jax.random.fold_in(key, 102)
    base = jax.random.normal(inner, (E, D, 2, FF), jnp.float32)
    base = base * D ** (-0.5)
    return base[owner].astype(jnp.bfloat16)


def draw_down_proj(key, part):
    owner = expert_owner(key)
    inner = jax.random.fold_in(key, 103)
    base = jax.random.normal(inner, (E, FF, D), jnp.float32)
    base = base * FF ** (-0.5)
    return base[owner].astype(jnp.bfloat16)


def draw_residual(key, part):
    inner = jax.random.fold_in(key, 104)
    noise_key, row_key = jax.random.split(inner)
    columns = jnp.arange(D).astype(jnp.float32) / D
    noise = jnp.clip(jax.random.normal(noise_key, (TOKENS, D), jnp.float32), -3.5, 3.5)
    row_scale = 0.15 * jnp.exp(jax.random.uniform(row_key, (TOKENS, 1), jnp.float32, 0.0, jnp.log(10.0)))
    col_scale = 0.5 * jnp.exp(columns * jnp.log(3.0))
    return (noise * row_scale * col_scale[None, :]).astype(jnp.bfloat16)


def draw_page_table(key, part):
    inner = jax.random.fold_in(key, 105)
    order = jax.random.permutation(inner, TOTAL_PAGES)
    return order.reshape(SEQ_ALL, PAGES_SEQ).astype(jnp.int32)


def with_ends(drawn, key, low, top_value):
    longest = drawn.shape.index(max(drawn.shape))
    spots = []
    for shift in (0, 1):
        where = [jax.random.randint(jax.random.fold_in(key, axis), (), 0, length) for axis, length in enumerate(drawn.shape)]
        where[longest] = (where[longest] + shift) % drawn.shape[longest]
        spots.append(tuple(where))
    return drawn.at[spots[0]].set(low).at[spots[1]].set(top_value)


def levels(stream_key, shape, cuts, least, largest):
    def one(axis_at, parts):
        steps = jax.random.uniform(jax.random.fold_in(jax.random.fold_in(stream_key, 6), axis_at), (parts,), jnp.float32, least / len(cuts), largest / len(cuts))
        return jnp.repeat(jnp.exp(steps), shape[axis_at] // parts).reshape((-1,) + (1,) * (len(shape) - axis_at - 1))

    loudness = one(*cuts[0])
    for cut in cuts[1:]:
        loudness = loudness * one(*cut)
    return loudness


def length_profile(count, total, reach, lean):
    loads = [(1 << 20) // math.isqrt(standing ** lean) + 1 for standing in range(2, count + 1)]
    spare, given = total - reach - (count - 1), [1] * (count - 1)
    while spare > 0:
        free = [i for i in range(count - 1) if given[i] < reach]
        pool, remaining = sum([loads[i] for i in free]), spare
        for i in free:
            addition = min(reach - given[i], max(1, remaining * loads[i] // pool), spare)
            given[i] = given[i] + addition
            spare = spare - addition
    return np.array([reach] + given)


def uneven(rng, number_of, total, reach, lean):
    if number_of == 2:
        one = jax.random.randint(rng, (), max(1, total - reach), min(reach, total - 1) + 1)
        return jnp.stack([one, total - one])
    lengths = jnp.asarray(length_profile(number_of, total, reach, lean), jnp.int32)
    couples = (number_of - 1) // 2
    giver, receiver = lengths[1:1 + 2 * couples:2], lengths[2:2 + 2 * couples:2]
    room = jnp.minimum(giver - 1, reach - receiver)
    shifted = jax.random.randint(jax.random.fold_in(rng, 1), (couples,), 0, 1 << 20) % (room + 1)
    lengths = lengths.at[1:1 + 2 * couples:2].set(giver - shifted).at[2:2 + 2 * couples:2].set(receiver + shifted)
    return lengths[jax.random.permutation(jax.random.fold_in(rng, 2), number_of)]


def routed_block(key, own, number, rows, amount, top, bound, slope):
    ranking = jax.random.permutation(key, amount)
    heavy_load, common = load_shares(amount, rows * top, bound, slope, True), load_shares(amount, rows * top, bound, slope, False)
    places = jnp.arange(amount)

    def named(tallies, turn):
        used = int((tallies > 0).sum())
        fixed = max(1, used // 4)
        moved = fixed + (places - fixed + turn * (used - fixed)) % max(1, amount - fixed)
        return jnp.zeros((amount,), jnp.int32).at[ranking[jnp.where(places < fixed, places, moved)]].set(jnp.asarray(tallies, jnp.int32))

    tallies = jnp.where(number % 4 == 0, named(heavy_load, number // 4), named(common, number - number // 4 - 1))
    mixed = jax.random.permutation(jax.random.fold_in(own, 3), amount)
    giver, sink = mixed[0:amount // 2 * 2:2], mixed[1:amount // 2 * 2:2]
    room = jnp.minimum(tallies[giver] - 1, bound - tallies[sink]) // 2
    room = jnp.where((giver == ranking[0]) | (sink == ranking[0]) | (tallies[sink] == 0), 0, jnp.maximum(room, 0))
    moved = jax.random.randint(jax.random.fold_in(own, 4), (amount // 2,), 0, 1 << 20) % (room + 1)
    tallies = tallies.at[giver].add(-moved).at[sink].add(moved)
    labels = jnp.searchsorted(jnp.cumsum(tallies), jnp.arange(rows * top), side="right").astype(jnp.int32)
    listing = labels.reshape(top, rows).T
    listing = listing[jax.random.permutation(jax.random.fold_in(own, 1), rows)]
    turn = jax.random.randint(jax.random.fold_in(own, 2), (rows, 1), 0, top)
    return jnp.take_along_axis(listing, (jnp.arange(top)[None, :] + turn) % top, axis=1)


def load_shares(amount, total, reach, lean, full):
    weights = [(1 << 20) // math.isqrt(rank ** lean) + 1 for rank in range(1, amount + 1)]
    largest = reach if full else min(reach, max(-(-total // amount), total * weights[0] // sum(weights)))
    least = 1 if total - largest >= amount - 1 else 0
    holding, spare = [largest] + [least] * (amount - 1), total - largest - least * (amount - 1)
    while spare > 0:
        free = [i for i in range(1, amount) if holding[i] < largest] or [i for i in range(1, amount) if holding[i] < reach]
        mass, left = sum([weights[i] for i in free]), spare
        for i in free:
            more = min(reach - holding[i], max(1, left * weights[i] // mass), spare)
            holding[i] = holding[i] + more
            spare = spare - more
    return np.array(holding)


def gaussian(rng, dims, deviation, reach, pieces=(), kind=jnp.bfloat16):
    array = deviation * jax.random.normal(rng, dims, jnp.float32)
    if pieces:
        array = array * levels(rng, dims, pieces, -0.22, 0.18)
    return jnp.clip(array, -reach, reach).astype(kind)


def setup_inputs(seed: int = 0) -> dict:
    keys = jax.random.split(jax.random.key(seed), 15)
    attn_out = gaussian(keys[0], (TOKENS, D), 0.4, 6.0, ((0, 16), (1, 2)))
    residual = draw_residual(jax.random.fold_in(keys[14], 71), 0)
    out_proj = gaussian(keys[2], (D, D), D ** -0.5, 0.15625, ((1, 2),))
    gain_attn = jnp.clip(1.0 + 0.15 * jax.random.normal(keys[3], (D,), jnp.float32), 0.25, 1.75)
    routes_keys = jax.random.split(jax.random.fold_in(keys[4], 1), TOKENS // ROWS_DEV)
    routes_turns = jax.random.permutation(jax.random.fold_in(keys[4], 3), TOKENS // ROWS_DEV)
    routes = jax.vmap(lambda own, number: routed_block(jax.random.fold_in(keys[4], 2), own, number, ROWS_DEV, SLOTS, TOP, CAP, 1))(routes_keys, routes_turns).reshape((TOKENS, TOP))
    gate_weights = jnp.clip(jnp.exp(math.log(0.5) - 2.3025851 * jax.random.uniform(keys[5], (TOKENS, TOP), jnp.float32) ** levels(keys[5], (TOKENS, TOP), ((0, 16),), -0.2, 0.2)), 0.05, 0.5)
    gate_up = draw_gate_up(jax.random.fold_in(keys[14], 71), 0)
    down_proj = draw_down_proj(jax.random.fold_in(keys[14], 71), 0)
    gain_moe = jnp.clip(1.0 + 0.15 * jax.random.normal(keys[8], (D,), jnp.float32), 0.25, 1.75)
    kv_proj = gaussian(keys[9], (D, KV2), D ** -0.5, 0.15625, ((1, 2),))
    prompt_lens = uneven(keys[10], PROMPTS, PRE_DEV * N_DP, LONGEST, 2).astype(jnp.int32)
    decode_pos = with_ends(jax.random.randint(keys[11], (DECODES,), 0, MAXLEN), jax.random.fold_in(keys[11], 1), 0, MAXLEN - 1).astype(jnp.int32)
    page_table = draw_page_table(jax.random.fold_in(keys[14], 71), 0)
    kv_cache = gaussian(keys[13], (TOTAL_PAGES, PAGE, KV2), 1.0, 6.0, ((0, 16), (2, 2)))
    return dict(attn_out=attn_out, residual=residual, out_proj=out_proj, gain_attn=gain_attn, routes=routes, gate_weights=gate_weights, gate_up=gate_up, down_proj=down_proj, gain_moe=gain_moe, kv_proj=kv_proj, prompt_lens=prompt_lens, decode_pos=decode_pos, page_table=page_table, kv_cache=kv_cache)


NORM_EPS = 1e-05
ROPE_BASE = 10000.0

def row_places(row_ids, prompt_lens, decode_pos, page_table):
    prompts = prompt_lens.shape[0]
    decodes = decode_pos.shape[0]
    device = row_ids // ROWS_DEV
    within = row_ids % ROWS_DEV
    prefill = within < PRE_DEV
    stream = device * PRE_DEV + within
    seq_ends = jnp.cumsum(prompt_lens).astype(jnp.int32)
    seq_pre = lax.optimization_barrier(jnp.sum((seq_ends[None, :] <= stream[:, None]).astype(jnp.int32), axis=1))
    seq_pre = jnp.minimum(seq_pre, prompts - 1)
    seq_begin = lax.optimization_barrier(jnp.sum(jnp.where(jnp.arange(prompts, dtype=jnp.int32)[None, :] == seq_pre[:, None], (seq_ends - prompt_lens)[None, :], 0), axis=1))
    decode_ids = device * DEC_DEV + within - PRE_DEV
    decode_at = lax.optimization_barrier(jnp.sum(jnp.where(jnp.arange(decodes, dtype=jnp.int32)[None, :] == decode_ids[:, None], decode_pos[None, :], 0), axis=1))
    sequence = jnp.where(prefill, seq_pre, prompts + decode_ids)
    position = jnp.where(prefill, stream - seq_begin, decode_at).astype(jnp.int32)
    page_num = page_table.reshape(-1)[(sequence * PAGES_SEQ + position // PAGE).astype(jnp.int32)]
    return (position, (page_num * PAGE + position % PAGE).astype(jnp.int32))

def rotate_keys(values, position, key_mask):
    half_dim = HD // 2
    inverse = jnp.exp(-(jnp.arange(half_dim).astype(jnp.float32) * (2.0 / HD)) * jnp.log(jnp.float32(ROPE_BASE)))
    angles = position[:, None] * inverse[None, :]
    cosine_table = jnp.concatenate([jnp.cos(angles), jnp.cos(angles)], axis=1)
    sine_table = jnp.concatenate([jnp.sin(angles), jnp.sin(angles)], axis=1)
    first_half = values[:, :, :half_dim]
    second_half = values[:, :, half_dim:]
    turned = jnp.concatenate([-second_half, first_half], axis=2)
    rotated = values * cosine_table[:, None, :] + turned * sine_table[:, None, :]
    return jnp.where(key_mask[None, :, None], rotated, values)

def rms_scale(values_f, gain):
    squares = lax.optimization_barrier(jnp.sum(values_f * values_f, axis=1, keepdims=True))
    return values_f * lax.rsqrt(squares / D + NORM_EPS) * gain[None, :]

def reference(attn_out, residual, out_proj, gain_attn, routes, gate_weights, gate_up, down_proj, gain_moe, kv_proj, prompt_lens, decode_pos, page_table, kv_cache):
    hidden_res = lax.optimization_barrier((residual.astype(jnp.float32) + jnp.dot(attn_out, out_proj, preferred_element_type=jnp.float32)).astype(jnp.bfloat16))
    res_f = hidden_res.astype(jnp.float32)
    normed = rms_scale(res_f, gain_attn).astype(jnp.bfloat16)
    slot_total = gate_up.shape[0]
    cap_all = N_DP * CAP
    block_width = D // N_MP
    flat_routes = routes.reshape(-1)
    flat_gates = jnp.concatenate([gate_weights.reshape(-1), jnp.zeros((1,), jnp.float32)])

    def per_slot(mixture, inputs):
        slot_id, slot_gu, slot_down = inputs
        found = jnp.nonzero(flat_routes == slot_id, size=cap_all, fill_value=TOKENS * TOP)[0].astype(jnp.int32)
        token_ids = (found // TOP).astype(jnp.int32)
        chosen = normed[jnp.minimum(token_ids, TOKENS - 1)]
        blocks = chosen.astype(jnp.float32).reshape(cap_all, N_MP, block_width)
        weight_blocks = slot_gu.astype(jnp.float32).reshape(N_MP, block_width, 2 * FF)
        partial_value = jnp.einsum('rmd,mdf->rmf', blocks, weight_blocks, precision=lax.Precision.HIGHEST)
        partial_value = lax.optimization_barrier(partial_value.astype(jnp.bfloat16))
        summed = lax.optimization_barrier(jnp.sum(partial_value.astype(jnp.float32), axis=1))
        activation = (jax.nn.silu(summed[:, :FF]) * summed[:, FF:]).astype(jnp.bfloat16)
        expert_out = jnp.dot(activation, slot_down, preferred_element_type=jnp.float32).astype(jnp.bfloat16)
        contrib = flat_gates[found][:, None] * expert_out.astype(jnp.float32)
        return (mixture.at[token_ids].add(contrib, mode='drop'), None)
    mixture, unused_out = lax.scan(per_slot, jnp.zeros((TOKENS, D), jnp.float32), (jnp.arange(slot_total, dtype=jnp.int32), gate_up, down_proj))
    layer_out = lax.optimization_barrier((res_f + mixture).astype(jnp.bfloat16))
    normed_kv = rms_scale(layer_out.astype(jnp.float32), gain_moe).astype(jnp.bfloat16)
    kv_full = jnp.dot(normed_kv, kv_proj, preferred_element_type=jnp.float32).reshape(TOKENS, 2 * KVH, HD)
    row_ids = jnp.arange(TOKENS, dtype=jnp.int32)
    position, linear = row_places(row_ids, prompt_lens, decode_pos, page_table)
    key_mask = jnp.arange(2 * KVH) < KVH
    rotated = rotate_keys(kv_full, position.astype(jnp.float32), key_mask).reshape(TOKENS, KV2).astype(jnp.bfloat16)
    flat_cache = kv_cache.reshape(TOTAL_PAGES * PAGE, KV2).at[linear].set(rotated)
    return (layer_out, flat_cache.reshape(kv_cache.shape))
```

```python
import functools
import jax
import jax.numpy as jnp
from jax import lax
from jax.experimental import pallas as pl
from jax.experimental.pallas import tpu as pltpu
from jax.sharding import PartitionSpec as P

D = 1536
TOP = 8
KVH = 8
HD = 64
PAGE = 128
PAGES_SEQ = 8
DEC_DEV = 2
ROWS_DEV = 192
PRE_DEV = 190


NORM_EPS = 1e-05
ROPE_BASE = 10000.0


def row_places(row_ids, prompt_lens, decode_pos, page_table):
    prompts = prompt_lens.shape[0]
    decodes = decode_pos.shape[0]
    device = row_ids // ROWS_DEV
    within = row_ids % ROWS_DEV
    prefill = within < PRE_DEV
    stream = device * PRE_DEV + within
    seq_ends = jnp.cumsum(prompt_lens)
    seq_pre = jnp.sum((seq_ends[None, :] <= stream[:, None]).astype(jnp.int32), axis=1)
    seq_pre = jnp.minimum(seq_pre, prompts - 1)
    seq_begin = jnp.sum(
        jnp.where(
            jnp.arange(prompts, dtype=jnp.int32)[None, :] == seq_pre[:, None],
            (seq_ends - prompt_lens)[None, :],
            0,
        ),
        axis=1,
    )
    decode_ids = device * DEC_DEV + within - PRE_DEV
    decode_at = jnp.sum(
        jnp.where(
            jnp.arange(decodes, dtype=jnp.int32)[None, :] == decode_ids[:, None],
            decode_pos[None, :],
            0,
        ),
        axis=1,
    )
    sequence = jnp.where(prefill, seq_pre, prompts + decode_ids)
    position = jnp.where(prefill, stream - seq_begin, decode_at)
    page_num = page_table.reshape(-1)[sequence * PAGES_SEQ + position // PAGE]
    return (position, page_num * PAGE + position % PAGE)


def rotate_keys(values, position, key_mask):
    half_dim = HD // 2
    inverse = jnp.exp(
        -(jnp.arange(half_dim).astype(jnp.float32) * (2.0 / HD)) * jnp.log(jnp.float32(ROPE_BASE))
    )
    angles = position[:, None] * inverse[None, :]
    cosine_table = jnp.concatenate([jnp.cos(angles), jnp.cos(angles)], axis=1)
    sine_table = jnp.concatenate([jnp.sin(angles), jnp.sin(angles)], axis=1)
    first_half = values[:, :, :half_dim]
    second_half = values[:, :, half_dim:]
    turned = jnp.concatenate([-second_half, first_half], axis=2)
    rotated = values * cosine_table[:, None, :] + turned * sine_table[:, None, :]
    return jnp.where(key_mask[None, :, None], rotated, values)


def fold_with(weight, block_in):
    return jnp.dot(block_in, weight, preferred_element_type=jnp.float32)


def on_device(
    attn_out,
    residual,
    out_proj,
    gain_attn,
    routes,
    gate_weights,
    gate_up,
    down_proj,
    gain_moe,
    kv_proj,
    prompt_lens,
    decode_pos,
    page_table,
    kv_cache,
):
    rows_here = attn_out.shape[0]
    dev_count = lax.axis_size("dp")
    my_dev = lax.axis_index("dp")
    my_col = lax.axis_index("mp")
    projected = fold_with(out_proj, lax.all_gather(attn_out, "mp", axis=1, tiled=True))
    hidden_res = lax.optimization_barrier(
        (residual.astype(jnp.float32) + projected).astype(jnp.bfloat16)
    )
    res_f = hidden_res.astype(jnp.float32)
    squares = lax.psum(jnp.sum(res_f * res_f, axis=1), "mp")
    normed = (res_f * lax.rsqrt(squares / D + NORM_EPS)[:, None] * gain_attn[None, :]).astype(
        jnp.bfloat16
    )
    slots_here = gate_up.shape[0]
    slot_total = slots_here * dev_count
    capacity = (5 * rows_here * TOP + 4 * slot_total - 1) // (4 * slot_total)
    width_here = normed.shape[1]
    flat_routes = routes.reshape(-1)
    onehot = (flat_routes[:, None] == jnp.arange(slot_total, dtype=jnp.int32)[None, :]).astype(
        jnp.int32
    )
    earlier = jnp.sum((jnp.cumsum(onehot, axis=0) - onehot) * onehot, axis=1)
    target = flat_routes * capacity + earlier
    outgoing = (
        jnp.zeros((slot_total * capacity, width_here), jnp.bfloat16)
        .at[target]
        .set(jnp.repeat(normed, TOP, axis=0))
    )
    arrived = lax.all_to_all(
        outgoing.reshape(dev_count, slots_here * capacity, width_here),
        "dp",
        split_axis=0,
        concat_axis=0,
        tiled=True,
    )
    expert_in = (
        arrived.reshape(dev_count, slots_here, capacity, width_here)
        .transpose(1, 0, 2, 3)
        .reshape(slots_here, dev_count * capacity, width_here)
    )
    partial_value = jnp.einsum(
        "srd,sdgf->srgf", expert_in, gate_up, preferred_element_type=jnp.float32
    ).astype(jnp.bfloat16)
    summed = lax.psum(partial_value, "mp").astype(jnp.float32)
    activation = (jax.nn.silu(summed[:, :, 0]) * summed[:, :, 1]).astype(jnp.bfloat16)
    expert_out = jnp.einsum(
        "srf,sfd->srd", activation, down_proj, preferred_element_type=jnp.float32
    ).astype(jnp.bfloat16)
    outbound = (
        expert_out.reshape(slots_here, dev_count, capacity, width_here)
        .transpose(1, 0, 2, 3)
        .reshape(dev_count, slots_here * capacity, width_here)
    )
    returned = lax.all_to_all(outbound, "dp", split_axis=0, concat_axis=0, tiled=True).reshape(
        slot_total * capacity, width_here
    )
    picked = returned[target].astype(jnp.float32)
    mixture = jnp.sum(
        (gate_weights.reshape(-1, 1) * picked).reshape(rows_here, TOP, width_here), axis=1
    )
    layer_out = lax.optimization_barrier((res_f + mixture).astype(jnp.bfloat16))
    out_f = layer_out.astype(jnp.float32)
    out_squares = lax.psum(jnp.sum(out_f * out_f, axis=1), "mp")
    normed_kv = (out_f * lax.rsqrt(out_squares / D + NORM_EPS)[:, None] * gain_moe[None, :]).astype(
        jnp.bfloat16
    )
    kv_local = fold_with(kv_proj, lax.all_gather(normed_kv, "mp", axis=1, tiled=True))
    heads_here = kv_proj.shape[1] // HD
    head_ids = my_col * heads_here + jnp.arange(heads_here, dtype=jnp.int32)
    row_ids = my_dev * rows_here + jnp.arange(rows_here, dtype=jnp.int32)
    position, linear = row_places(row_ids, prompt_lens, decode_pos, page_table)
    rotated = rotate_keys(
        kv_local.reshape(rows_here, heads_here, HD), position.astype(jnp.float32), head_ids < KVH
    )
    rotated = rotated.reshape(rows_here, kv_proj.shape[1]).astype(jnp.bfloat16)
    per_dev = kv_cache.shape[0] * kv_cache.shape[1]
    flat_cache = kv_cache.reshape(per_dev, kv_cache.shape[2])
    new_slots = lax.all_gather(linear, "dp", axis=0, tiled=True)
    is_mine = new_slots // per_dev == my_dev
    local_slot = jnp.where(is_mine, new_slots % per_dev, per_dev)
    written = flat_cache.at[local_slot].set(
        lax.all_gather(rotated, "dp", axis=0, tiled=True), mode="drop"
    )
    return (layer_out, written.reshape(kv_cache.shape))


NZ = 4
NX = 2
NC = 2
BF = jnp.bfloat16
F32 = jnp.float32
Z_ORDER = (0, 1, 3, 2)


def at(z, x, c):
    return (z * NX + x) * NC + c


def moves(dz, dx, dc):
    return [
        (at(z, x, c), at((z + dz) % NZ, x ^ dx, c ^ dc))
        for z in range(NZ)
        for x in range(NX)
        for c in range(NC)
    ]


def z_move(value, dz):
    return lax.ppermute(value, "dp", moves(dz, 0, 0))


def x_move(value):
    return lax.ppermute(value, "dp", moves(0, 1, 0))


def core_move(value):
    return lax.ppermute(value, "dp", moves(0, 0, 1))


def y_move(value):
    return lax.ppermute(value, "mp", [(0, 1), (1, 0)])


def gate_up_kernel(col_ref, a0, a1, b0, b1, pick_ref, w_ref, send_ref, keep_ref, rows):
    cap = pick_ref.shape[2]
    for i, block in enumerate((a0, a1, b0, b1)):
        rows[i * cap : (i + 1) * cap, :] = jnp.dot(
            pick_ref[0, i], block[...], preferred_element_type=F32
        )
    part = jnp.dot(rows[...].astype(BF), w_ref[0], preferred_element_type=F32)
    first, second = part[: 2 * cap], part[2 * cap :]
    keeps_first = col_ref[0] == 0
    send_ref[0] = jnp.where(keeps_first, second, first).astype(BF)
    keep_ref[0] = jnp.where(keeps_first, first, second)


def gate_up(col, blocks, pick, weight):
    slots, _, cap, rows = pick.shape
    width, hidden2 = weight.shape[1], weight.shape[2]
    whole = pl.BlockSpec((rows, width), lambda s, c: (0, 0))
    out = pl.BlockSpec((1, 2 * cap, hidden2), lambda s, c: (s, 0, 0))
    return pl.pallas_call(
        gate_up_kernel,
        out_shape=(
            jax.ShapeDtypeStruct((slots, 2 * cap, hidden2), BF),
            jax.ShapeDtypeStruct((slots, 2 * cap, hidden2), F32),
        ),
        grid_spec=pltpu.PrefetchScalarGridSpec(
            num_scalar_prefetch=1,
            grid=(slots,),
            in_specs=[whole] * 4
            + [
                pl.BlockSpec((1, 4, cap, rows), lambda s, c: (s, 0, 0, 0)),
                pl.BlockSpec((1, width, hidden2), lambda s, c: (s, 0, 0)),
            ],
            out_specs=(out, out),
            scratch_shapes=[pltpu.VMEM((4 * cap, width), F32)],
        ),
        cost_estimate=pl.CostEstimate(
            flops=2 * slots * 4 * cap * width * hidden2, bytes_accessed=8 << 20, transcendentals=0
        ),
        name="gate_up",
    )(col, *blocks, pick, weight)


def act_kernel(keep_ref, got_ref, gate_ref, act_ref):
    total = keep_ref[...] + got_ref[...].astype(F32)
    half = total.shape[2] // 2
    act_ref[...] = (jax.nn.silu(total[:, :, :half]) * total[:, :, half:] * gate_ref[...]).astype(BF)


def activate(keep, got, gate):
    slots, rows, hidden2 = keep.shape
    return pl.pallas_call(
        act_kernel,
        out_shape=jax.ShapeDtypeStruct((slots, rows, hidden2 // 2), BF),
        cost_estimate=pl.CostEstimate(
            flops=10 * keep.size, bytes_accessed=2 << 20, transcendentals=keep.size
        ),
        name="activate",
    )(keep, got, gate)


def down_kernel(col_ref, mine_ref, got_ref, spread_ref, w_ref, a0, a1, b0, b1, rows):
    s = pl.program_id(0)
    cap = mine_ref.shape[1] // 2
    keeps_first = col_ref[0] == 0
    mine, got = mine_ref[0], got_ref[0]
    first = jnp.where(keeps_first, mine, got)
    second = jnp.where(keeps_first, got, mine)
    for half, act in enumerate((first, second)):
        done = jnp.dot(act, w_ref[0], preferred_element_type=F32)
        for i in range(2):
            rows[2 * half + i, pl.ds(pl.multiple_of(s * cap, 8), cap), :] = done[
                i * cap : (i + 1) * cap
            ]

    @pl.when(s == pl.num_programs(0) - 1)
    def _():
        for i, out in enumerate((a0, a1, b0, b1)):
            out[...] = jnp.dot(
                spread_ref[i], rows[i].astype(BF), preferred_element_type=F32
            ).astype(BF)


def down(col, mine, got, spread, weight):
    slots, half_rows, hidden = mine.shape
    cap = half_rows // 2
    width = weight.shape[2]
    tokens = spread.shape[1]
    act_spec = pl.BlockSpec((1, half_rows, hidden), lambda s, c: (s, 0, 0))
    out = pl.BlockSpec((tokens, width), lambda s, c: (0, 0))
    return pl.pallas_call(
        down_kernel,
        out_shape=[jax.ShapeDtypeStruct((tokens, width), BF)] * 4,
        grid_spec=pltpu.PrefetchScalarGridSpec(
            num_scalar_prefetch=1,
            grid=(slots,),
            in_specs=[
                act_spec,
                act_spec,
                pl.BlockSpec((4, tokens, slots * cap), lambda s, c: (0, 0, 0)),
                pl.BlockSpec((1, hidden, width), lambda s, c: (s, 0, 0)),
            ],
            out_specs=[out] * 4,
            scratch_shapes=[pltpu.VMEM((4, slots * cap, width), F32)],
        ),
        cost_estimate=pl.CostEstimate(
            flops=4 * slots * half_rows * width * hidden, bytes_accessed=4 << 20, transcendentals=0
        ),
        name="down",
    )(col, mine, got, spread, weight)


def page_kernel(place_ref, page_ref, *refs):
    count = len(refs) - 3
    cache_ref, out_ref, everything = refs[count], refs[count + 1], refs[count + 2]

    @pl.when(pl.program_id(0) == 0)
    def _():
        for i in range(count):
            everything[place_ref[i]] = refs[i][...]

    pages, length, _ = cache_ref.shape
    tokens = everything.shape[1]
    i = lax.broadcasted_iota(jnp.int32, (length, 2 * tokens), 0)
    m = lax.broadcasted_iota(jnp.int32, (length, 2 * tokens), 1)
    row = lax.broadcasted_iota(jnp.int32, (length, 1), 0)
    for k in range(pages):
        page = pl.program_id(0) * pages + k
        base, offset = page_ref[0, page], page_ref[1, page]
        low, high, skip = page_ref[2, page], page_ref[3, page], page_ref[4, page]

        @pl.when(high > low)
        def _():
            source = i + offset + jnp.where(i + offset >= PRE_DEV, skip, 0)
            select = (m == source).astype(F32).astype(BF)
            taken = jnp.dot(
                select[:, :tokens], everything[base], preferred_element_type=F32
            ) + jnp.dot(
                select[:, tokens:],
                everything[jnp.minimum(base + 1, count - 1)],
                preferred_element_type=F32,
            )
            hit = (row >= low) & (row < high)
            out_ref[k] = jnp.where(hit, taken, cache_ref[k].astype(F32)).astype(BF)

        @pl.when(high <= low)
        def _():
            out_ref[k] = cache_ref[k]


def write_pages(place, page_data, blocks, cache):
    pages, length, width = cache.shape
    step = 4 if pages % 4 == 0 else 1
    tokens = blocks[0].shape[0]
    whole = pl.BlockSpec((tokens, width), lambda s, a, b: (0, 0))
    page_spec = pl.BlockSpec((step, length, width), lambda s, a, b: (s, 0, 0))
    return pl.pallas_call(
        page_kernel,
        out_shape=jax.ShapeDtypeStruct(cache.shape, cache.dtype),
        grid_spec=pltpu.PrefetchScalarGridSpec(
            num_scalar_prefetch=2,
            grid=(pages // step,),
            in_specs=[whole] * len(blocks) + [page_spec],
            out_specs=page_spec,
            scratch_shapes=[pltpu.VMEM((len(blocks), tokens, width), cache.dtype)],
        ),
        name="write_pages",
    )(place, page_data, *blocks, cache)


def page_sources(my_dev, pages_here, prompt_lens, decode_pos, page_table):
    prompts = prompt_lens.shape[0]
    ends = jnp.cumsum(prompt_lens)
    ordinal = jnp.arange(PAGES_SEQ, dtype=jnp.int32)[None, :]
    start = (ends - prompt_lens)[:, None] + ordinal * PAGE
    high_p = jnp.clip(prompt_lens[:, None] - ordinal * PAGE, 0, PAGE)
    base_p = start // PRE_DEV
    offset_p = start % PRE_DEV
    c = jnp.arange(decode_pos.shape[0], dtype=jnp.int32)[:, None]
    at_row = (decode_pos % PAGE)[:, None] + 0 * ordinal
    hit = (decode_pos // PAGE)[:, None] == ordinal
    base_d = c // DEC_DEV + 0 * ordinal
    offset_d = PRE_DEV + c % DEC_DEV - at_row
    high_d = jnp.where(hit, at_row + 1, at_row)
    both = lambda p, d: jnp.concatenate([p, d], axis=0).reshape(-1)
    entries = jnp.stack(
        [
            both(base_p, base_d),
            both(offset_p, offset_d),
            both(0 * high_p, at_row),
            both(high_p, high_d),
            both(0 * high_p + DEC_DEV, 0 * high_d),
        ]
    )
    entries = entries.at[0].set(jnp.where(entries[3] > entries[2], entries[0], 0))
    mine = my_dev * pages_here + jnp.arange(pages_here, dtype=jnp.int32)
    match = page_table.reshape(-1)[None, :] == mine[:, None]
    return jnp.sum(jnp.where(match[None], entries[:, None, :], 0), axis=2).astype(jnp.int32)


def routing(meta, slot_ids, cap):
    names, gates = meta[:, :TOP], meta[:, TOP:]
    rows = meta.shape[2]
    same = names[:, None] == slot_ids.astype(F32)[None, :, None, None]
    chosen = jnp.max(same.astype(F32), axis=2)
    gate = jnp.sum(jnp.where(same, gates[:, None], 0.0), axis=2)
    r = jnp.arange(rows, dtype=jnp.int32)
    before = (r[:, None] < r[None, :]).astype(BF)
    position = jnp.einsum("bst,tu->bsu", chosen.astype(BF), before, preferred_element_type=F32)
    position = jnp.where(chosen > 0, position, -1.0)
    places = jnp.arange(cap, dtype=jnp.int32).astype(F32)
    taken = position[:, :, None, :] == places[None, None, :, None]
    pick = taken.astype(BF).transpose(1, 0, 2, 3)
    slots = slot_ids.shape[0]
    wide = jnp.repeat(position.transpose(0, 2, 1), cap, axis=2)
    spread = (wide == jnp.tile(places, slots)[None, None, :]).astype(BF)
    row_gate = jnp.sum(jnp.where(taken, gate[:, :, None, :], 0.0), axis=3)
    return pick, spread, row_gate.transpose(1, 0, 2)


def on_device_16x2(
    attn_out,
    residual,
    out_proj,
    gain_attn,
    routes,
    gate_weights,
    gate_up_w,
    down_proj,
    gain_moe,
    kv_proj,
    prompt_lens,
    decode_pos,
    page_table,
    kv_cache,
):
    rows_here, width = attn_out.shape
    my_dev = lax.axis_index("dp")
    my_col = lax.axis_index("mp")
    col = my_col.reshape(1)
    slots_here = gate_up_w.shape[0]
    slot_total = slots_here * NZ * NX * NC
    cap = (5 * rows_here * TOP + 4 * slot_total - 1) // (4 * slot_total)
    weight = gate_up_w.reshape(slots_here, width, -1)

    attn_other = y_move(attn_out)
    meta = jnp.concatenate([routes.astype(F32).T, gate_weights.T], axis=0)
    meta_x = x_move(meta)
    pair = jnp.stack([meta, meta_x])
    quad = jnp.concatenate([pair, core_move(pair)])
    metas = {0: quad}
    for dz in (1, 3, 2):
        metas[dz] = z_move(quad, dz)

    own_first = lambda w: (
        lax.dynamic_slice_in_dim(w, my_col * width, width, 0),
        lax.dynamic_slice_in_dim(w, (1 - my_col) * width, width, 0),
    )
    proj_own, proj_other = own_first(out_proj)
    dot = functools.partial(jnp.dot, preferred_element_type=F32)
    hidden = (
        residual.astype(F32) + dot(attn_out, proj_own) + dot(attn_other, proj_other)
    ).astype(BF)
    hidden = lax.optimization_barrier(hidden)
    res_f = hidden.astype(F32)
    squares = jnp.sum(res_f * res_f, axis=1)
    squares = squares + y_move(squares)
    normed = (res_f * lax.rsqrt(squares / D + NORM_EPS)[:, None] * gain_attn[None, :]).astype(BF)

    slot_ids = my_dev * slots_here + jnp.arange(slots_here, dtype=jnp.int32)
    routed = {dz: routing(metas[dz], slot_ids, cap) for dz in range(NZ)}

    column = {dz: z_move(normed, dz) if dz else normed for dz in Z_ORDER}
    blocks = {}
    for dz in Z_ORDER:
        a0 = column[dz]
        a1 = x_move(a0)
        blocks[dz] = (a0, a1, core_move(a0), core_move(a1))

    mixture = res_f
    for dz in Z_ORDER:
        pick, spread, row_gate = routed[dz]
        send, keep = gate_up(col, blocks[dz], pick, weight)
        got = y_move(send)
        gate = jnp.where(my_col == 0, row_gate[:, :2], row_gate[:, 2:])
        act = activate(keep, got, gate.reshape(slots_here, 2 * cap, 1))
        act_got = y_move(act)
        a0, a1, b0, b1 = down(col, act, act_got, spread, down_proj)
        a1 = (a1.astype(F32) + core_move(b1).astype(F32)).astype(BF)
        from_x = x_move(a1).astype(F32)
        a0 = a0.astype(F32) + core_move(b0).astype(F32) + from_x
        mixture = mixture + (z_move(a0.astype(BF), NZ - dz).astype(F32) if dz else a0)
    layer_out = lax.optimization_barrier(mixture.astype(BF))

    out_other = y_move(layer_out)
    gain_other = y_move(gain_moe)
    own_f, other_f = layer_out.astype(F32), out_other.astype(F32)
    out_squares = jnp.sum(own_f * own_f, axis=1) + jnp.sum(other_f * other_f, axis=1)
    scale = lax.rsqrt(out_squares / D + NORM_EPS)[:, None]
    v_own = (own_f * scale * gain_moe[None, :]).astype(BF)
    v_other = (other_f * scale * gain_other[None, :]).astype(BF)

    columns = kv_proj.shape[1]
    halves = kv_proj.reshape(-1, columns // HD, 2, HD // 2)
    turned = jnp.stack([-halves[:, :, 1], halves[:, :, 0]], axis=2).reshape(kv_proj.shape)
    kv_own, kv_other = own_first(jnp.concatenate([kv_proj, turned], axis=1))
    both = dot(v_own, kv_own) + dot(v_other, kv_other)
    row_ids = my_dev * rows_here + jnp.arange(rows_here, dtype=jnp.int32)
    position, _ = row_places(row_ids, prompt_lens, decode_pos, page_table)
    lane = jnp.arange(columns, dtype=jnp.int32)
    inverse = jnp.exp(-((lane % (HD // 2)).astype(F32) * (2.0 / HD)) * jnp.log(F32(ROPE_BASE)))
    angles = position.astype(F32)[:, None] * inverse[None, :]
    is_key = (my_col * columns + lane < KVH * HD)[None, :]
    cosine = jnp.where(is_key, jnp.cos(angles), 1.0)
    sine = jnp.where(is_key, jnp.sin(angles), 0.0)
    rotated = (both[:, :columns] * cosine + both[:, columns:] * sine).astype(BF)

    z, x, c = my_dev // (NX * NC), my_dev // NC % NX, my_dev % NC
    kv_blocks, places = [], []
    kv_column = {dz: z_move(rotated, dz) if dz else rotated for dz in Z_ORDER}
    for dz in Z_ORDER:
        a0 = kv_column[dz]
        a1 = x_move(a0)
        kv_blocks += [a0, a1, core_move(a0), core_move(a1)]
        source_z = (z + NZ - dz) % NZ
        places += [at(source_z, x, c), at(source_z, 1 - x, c), at(source_z, x, 1 - c), at(source_z, 1 - x, 1 - c)]
    page_data = page_sources(my_dev, kv_cache.shape[0], prompt_lens, decode_pos, page_table)
    written = write_pages(jnp.stack(places).astype(jnp.int32), page_data, kv_blocks, kv_cache)
    return (layer_out, written)


def solution(mesh):
    body = on_device_16x2 if (mesh.shape["dp"], mesh.shape["mp"]) == (NZ * NX * NC, 2) else on_device
    placed = (
        P("dp", "mp"),
        P("dp", "mp"),
        P(None, "mp"),
        P("mp"),
        P("dp", None),
        P("dp", None),
        P("dp", "mp", None, None),
        P("dp", None, "mp"),
        P("mp"),
        P(None, "mp"),
        P(),
        P(),
        P(),
        P("dp", None, "mp"),
    )
    return jax.shard_map(
        body,
        mesh=mesh,
        in_specs=placed,
        out_specs=(P("dp", "mp"), P("dp", None, "mp")),
        check_vma=False,
    )
```

```python
import functools
import jax
import jax.numpy as jnp
from jax import lax
from jax.experimental import pallas as pl
from jax.experimental.pallas import tpu as pltpu
from jax.sharding import PartitionSpec as P

D = 1536
TOP = 8
KVH = 8
HD = 64
PAGE = 128
PAGES_SEQ = 8
DEC_DEV = 2
ROWS_DEV = 192
PRE_DEV = 190


NORM_EPS = 1e-05
ROPE_BASE = 10000.0


def row_places(row_ids, prompt_lens, decode_pos, page_table):
    prompts = prompt_lens.shape[0]
    decodes = decode_pos.shape[0]
    device = row_ids // ROWS_DEV
    within = row_ids % ROWS_DEV
    prefill = within < PRE_DEV
    stream = device * PRE_DEV + within
    seq_ends = jnp.cumsum(prompt_lens)
    seq_pre = jnp.sum((seq_ends[None, :] <= stream[:, None]).astype(jnp.int32), axis=1)
    seq_pre = jnp.minimum(seq_pre, prompts - 1)
    seq_begin = jnp.sum(
        jnp.where(
            jnp.arange(prompts, dtype=jnp.int32)[None, :] == seq_pre[:, None],
            (seq_ends - prompt_lens)[None, :],
            0,
        ),
        axis=1,
    )
    decode_ids = device * DEC_DEV + within - PRE_DEV
    decode_at = jnp.sum(
        jnp.where(
            jnp.arange(decodes, dtype=jnp.int32)[None, :] == decode_ids[:, None],
            decode_pos[None, :],
            0,
        ),
        axis=1,
    )
    sequence = jnp.where(prefill, seq_pre, prompts + decode_ids)
    position = jnp.where(prefill, stream - seq_begin, decode_at)
    page_num = page_table.reshape(-1)[sequence * PAGES_SEQ + position // PAGE]
    return (position, page_num * PAGE + position % PAGE)


def rotate_keys(values, position, key_mask):
    half_dim = HD // 2
    inverse = jnp.exp(
        -(jnp.arange(half_dim).astype(jnp.float32) * (2.0 / HD)) * jnp.log(jnp.float32(ROPE_BASE))
    )
    angles = position[:, None] * inverse[None, :]
    cosine_table = jnp.concatenate([jnp.cos(angles), jnp.cos(angles)], axis=1)
    sine_table = jnp.concatenate([jnp.sin(angles), jnp.sin(angles)], axis=1)
    first_half = values[:, :, :half_dim]
    second_half = values[:, :, half_dim:]
    turned = jnp.concatenate([-second_half, first_half], axis=2)
    rotated = values * cosine_table[:, None, :] + turned * sine_table[:, None, :]
    return jnp.where(key_mask[None, :, None], rotated, values)


def fold_with(weight, block_in):
    return jnp.dot(block_in, weight, preferred_element_type=jnp.float32)


def on_device(
    attn_out,
    residual,
    out_proj,
    gain_attn,
    routes,
    gate_weights,
    gate_up,
    down_proj,
    gain_moe,
    kv_proj,
    prompt_lens,
    decode_pos,
    page_table,
    kv_cache,
):
    rows_here = attn_out.shape[0]
    dev_count = lax.axis_size("dp")
    my_dev = lax.axis_index("dp")
    my_col = lax.axis_index("mp")
    projected = fold_with(out_proj, lax.all_gather(attn_out, "mp", axis=1, tiled=True))
    hidden_res = lax.optimization_barrier(
        (residual.astype(jnp.float32) + projected).astype(jnp.bfloat16)
    )
    res_f = hidden_res.astype(jnp.float32)
    squares = lax.psum(jnp.sum(res_f * res_f, axis=1), "mp")
    normed = (res_f * lax.rsqrt(squares / D + NORM_EPS)[:, None] * gain_attn[None, :]).astype(
        jnp.bfloat16
    )
    slots_here = gate_up.shape[0]
    slot_total = slots_here * dev_count
    capacity = (5 * rows_here * TOP + 4 * slot_total - 1) // (4 * slot_total)
    width_here = normed.shape[1]
    flat_routes = routes.reshape(-1)
    onehot = (flat_routes[:, None] == jnp.arange(slot_total, dtype=jnp.int32)[None, :]).astype(
        jnp.int32
    )
    earlier = jnp.sum((jnp.cumsum(onehot, axis=0) - onehot) * onehot, axis=1)
    target = flat_routes * capacity + earlier
    outgoing = (
        jnp.zeros((slot_total * capacity, width_here), jnp.bfloat16)
        .at[target]
        .set(jnp.repeat(normed, TOP, axis=0))
    )
    arrived = lax.all_to_all(
        outgoing.reshape(dev_count, slots_here * capacity, width_here),
        "dp",
        split_axis=0,
        concat_axis=0,
        tiled=True,
    )
    expert_in = (
        arrived.reshape(dev_count, slots_here, capacity, width_here)
        .transpose(1, 0, 2, 3)
        .reshape(slots_here, dev_count * capacity, width_here)
    )
    partial_value = jnp.einsum(
        "srd,sdgf->srgf", expert_in, gate_up, preferred_element_type=jnp.float32
    ).astype(jnp.bfloat16)
    summed = lax.psum(partial_value, "mp").astype(jnp.float32)
    activation = (jax.nn.silu(summed[:, :, 0]) * summed[:, :, 1]).astype(jnp.bfloat16)
    expert_out = jnp.einsum(
        "srf,sfd->srd", activation, down_proj, preferred_element_type=jnp.float32
    ).astype(jnp.bfloat16)
    outbound = (
        expert_out.reshape(slots_here, dev_count, capacity, width_here)
        .transpose(1, 0, 2, 3)
        .reshape(dev_count, slots_here * capacity, width_here)
    )
    returned = lax.all_to_all(outbound, "dp", split_axis=0, concat_axis=0, tiled=True).reshape(
        slot_total * capacity, width_here
    )
    picked = returned[target].astype(jnp.float32)
    mixture = jnp.sum(
        (gate_weights.reshape(-1, 1) * picked).reshape(rows_here, TOP, width_here), axis=1
    )
    layer_out = lax.optimization_barrier((res_f + mixture).astype(jnp.bfloat16))
    out_f = layer_out.astype(jnp.float32)
    out_squares = lax.psum(jnp.sum(out_f * out_f, axis=1), "mp")
    normed_kv = (out_f * lax.rsqrt(out_squares / D + NORM_EPS)[:, None] * gain_moe[None, :]).astype(
        jnp.bfloat16
    )
    kv_local = fold_with(kv_proj, lax.all_gather(normed_kv, "mp", axis=1, tiled=True))
    heads_here = kv_proj.shape[1] // HD
    head_ids = my_col * heads_here + jnp.arange(heads_here, dtype=jnp.int32)
    row_ids = my_dev * rows_here + jnp.arange(rows_here, dtype=jnp.int32)
    position, linear = row_places(row_ids, prompt_lens, decode_pos, page_table)
    rotated = rotate_keys(
        kv_local.reshape(rows_here, heads_here, HD), position.astype(jnp.float32), head_ids < KVH
    )
    rotated = rotated.reshape(rows_here, kv_proj.shape[1]).astype(jnp.bfloat16)
    per_dev = kv_cache.shape[0] * kv_cache.shape[1]
    flat_cache = kv_cache.reshape(per_dev, kv_cache.shape[2])
    new_slots = lax.all_gather(linear, "dp", axis=0, tiled=True)
    is_mine = new_slots // per_dev == my_dev
    local_slot = jnp.where(is_mine, new_slots % per_dev, per_dev)
    written = flat_cache.at[local_slot].set(
        lax.all_gather(rotated, "dp", axis=0, tiled=True), mode="drop"
    )
    return (layer_out, written.reshape(kv_cache.shape))


NZ = 4
NX = 2
NC = 2
BF = jnp.bfloat16
F32 = jnp.float32
GATE_LANES = 256
LIGHT = pl.CostEstimate(flops=1, bytes_accessed=1, transcendentals=0)
ROOM = pltpu.CompilerParams(vmem_limit_bytes=16 << 20)


def at(z, x, c):
    return (z * NX + x) * NC + c


def moves(dz, dx, dc):
    return [
        (at(z, x, c), at((z + dz) % NZ, x ^ dx, c ^ dc))
        for z in range(NZ)
        for x in range(NX)
        for c in range(NC)
    ]


def z_move(value, dz):
    return lax.ppermute(value, "dp", moves(dz, 0, 0))


def x_move(value):
    return lax.ppermute(value, "dp", moves(0, 1, 0))


def core_move(value):
    return lax.ppermute(value, "dp", moves(0, 0, 1))


def y_move(value):
    return lax.ppermute(value, "mp", [(0, 1), (1, 0)])


def after(value, *earlier):
    return lax.optimization_barrier((value,) + earlier)[0]


def picked(info, slots, cap):
    place = lax.broadcasted_iota(jnp.int32, (cap, info.shape[1]), 0).astype(F32)
    return jnp.concatenate([(info[q : q + 1] == place).astype(F32) for q in range(slots)], axis=0)


def gate_up_kernel(count, mine_ref, w_ref, *refs):
    *sources, send_ref, keep_ref, info_ref, rows = refs
    slots, total, _ = rows.shape
    cap = total // count
    s = pl.program_id(0)

    @pl.when(s == 0)
    def _():
        blocks = [b for r in sources for b in ([r] if len(r.shape) == 2 else [r.at[0], r.at[1]])]
        tokens = info_ref.shape[2]
        r = lax.broadcasted_iota(jnp.int32, (tokens, tokens), 0)
        before = (r < lax.broadcasted_iota(jnp.int32, (tokens, tokens), 1)).astype(F32).astype(BF)
        for i, block in enumerate(blocks):
            meta = block[tokens:, :].astype(F32)
            names = meta[:TOP, :tokens]
            gates = sum(meta[TOP:, k * GATE_LANES : k * GATE_LANES + tokens] for k in range(3))
            chosen, gate = [], []
            for q in range(slots):
                same = names == (mine_ref[1] + q).astype(F32)
                chosen.append(jnp.max(same.astype(F32), axis=0, keepdims=True))
                gate.append(jnp.sum(jnp.where(same, gates, 0.0), axis=0, keepdims=True))
            unused = jnp.zeros((info_ref.shape[1] - slots, tokens), F32)
            chosen = jnp.concatenate(chosen + [unused], axis=0)
            place = jnp.dot(chosen.astype(BF), before, preferred_element_type=F32)
            place = jnp.where(chosen > 0, place, -1.0)
            rest = jnp.zeros((info_ref.shape[1] - 2 * slots, tokens), F32)
            info_ref[i] = jnp.concatenate([place[:slots]] + gate + [rest], axis=0)
            pick = picked(place, slots, cap).astype(BF)
            taken = jnp.dot(pick, block[:tokens, :], preferred_element_type=F32)
            for q in range(slots):
                rows[q, i * cap : (i + 1) * cap] = taken[q * cap : (q + 1) * cap]

    x = rows[s].astype(BF)
    half, hidden = total // 2, w_ref.shape[3]
    keeps_first = mine_ref[0] == 0
    for k in range(2):
        part = jnp.dot(x, w_ref[k, 0], preferred_element_type=F32)
        first, second = part[:half], part[half:]
        send_ref[0, :, k * hidden : (k + 1) * hidden] = jnp.where(
            keeps_first, second, first
        ).astype(BF)
        keep_ref[0, :, k * hidden : (k + 1) * hidden] = jnp.where(keeps_first, first, second)


def gate_up(mine, blocks, weight, cap):
    _, slots, width, hidden = weight.shape
    n = sum(b.ndim - 1 for b in blocks)
    tokens = blocks[0].shape[-2] - 2 * TOP
    half = n * cap // 2
    info = (n, -(-2 * slots // 8) * 8, tokens)
    out = pl.BlockSpec((1, half, 2 * hidden), lambda s, c: (s, 0, 0))
    return pl.pallas_call(
        functools.partial(gate_up_kernel, n),
        out_shape=(
            jax.ShapeDtypeStruct((slots, half, 2 * hidden), BF),
            jax.ShapeDtypeStruct((slots, half, 2 * hidden), F32),
            jax.ShapeDtypeStruct(info, F32),
        ),
        grid_spec=pltpu.PrefetchScalarGridSpec(
            num_scalar_prefetch=1,
            grid=(slots,),
            in_specs=[pl.BlockSpec((2, 1, width, hidden), lambda s, c: (0, s, 0, 0))]
            + [pl.BlockSpec(b.shape, lambda s, c, d=b.ndim: (0,) * d) for b in blocks],
            out_specs=(out, out, pl.BlockSpec(info, lambda s, c: (0, 0, 0))),
            scratch_shapes=[pltpu.VMEM((slots, n * cap, width), F32)],
        ),
        cost_estimate=LIGHT,
        compiler_params=ROOM,
        name="gate_up",
    )(mine, weight, *blocks)


def act_kernel(col_ref, info_ref, keep_ref, got_ref, act_ref):
    s = pl.program_id(0)
    slots = pl.num_programs(0)
    n = info_ref.shape[0] // 2
    cap = keep_ref.shape[1] // n
    place = lax.broadcasted_iota(jnp.int32, (cap, info_ref.shape[2]), 0).astype(F32)
    gates = []
    for i in range(n):
        block = col_ref[0] * n + i
        position = info_ref[block, pl.ds(s, 1), :]
        gate = info_ref[block, pl.ds(slots + s, 1), :]
        gates.append(jnp.sum(jnp.where(position == place, gate, 0.0), axis=1, keepdims=True))
    gate = jnp.concatenate(gates, axis=0) if n > 1 else gates[0]
    total = keep_ref[0] + got_ref[0].astype(F32)
    half = total.shape[1] // 2
    act_ref[0] = (jax.nn.silu(total[:, :half]) * total[:, half:] * gate).astype(BF)


def activate(col, info, keep, got):
    slots, rows, hidden2 = keep.shape
    spec = lambda w: pl.BlockSpec((1, rows, w), lambda s, c: (s, 0, 0))
    return pl.pallas_call(
        act_kernel,
        out_shape=jax.ShapeDtypeStruct((slots, rows, hidden2 // 2), BF),
        grid_spec=pltpu.PrefetchScalarGridSpec(
            num_scalar_prefetch=1,
            grid=(slots,),
            in_specs=[
                pl.BlockSpec(info.shape, lambda s, c: (0, 0, 0)),
                spec(hidden2),
                spec(hidden2),
            ],
            out_specs=spec(hidden2 // 2),
        ),
        cost_estimate=LIGHT,
        compiler_params=ROOM,
        name="activate",
    )(col, info, keep, got)


def down_kernel(col_ref, info_ref, mine_ref, got_ref, w_ref, *refs):
    *outs, rows = refs
    s = pl.program_id(0)
    n = len(outs) // 2
    slots = pl.num_programs(0)
    total = rows.shape[1]
    count = info_ref.shape[0]
    cap = mine_ref.shape[1] // n
    keeps_first = col_ref[0] == 0
    mine, got = mine_ref[0], got_ref[0]
    for half, act in enumerate(
        (jnp.where(keeps_first, mine, got), jnp.where(keeps_first, got, mine))
    ):
        done = jnp.dot(act, w_ref[0], preferred_element_type=F32)
        for i in range(n):
            rows[half * n + i, pl.ds(pl.multiple_of(s * cap, 8), cap), :] = done[
                i * cap : (i + 1) * cap
            ]

    @pl.when(s == slots - 1)
    def _():
        for i in range(count):
            pick = picked(info_ref[i], total // cap, cap)
            summed = jnp.dot(pick.T.astype(BF), rows[i].astype(BF), preferred_element_type=F32)
            outs[i][...] = summed.astype(BF)


def down(col, info, mine, got, weight):
    slots, half_rows, hidden = mine.shape
    n = info.shape[0] // 2
    cap = half_rows // n
    tokens, width = info.shape[2], weight.shape[2]
    act_spec = pl.BlockSpec((1, half_rows, hidden), lambda s, c: (s, 0, 0))
    out = pl.BlockSpec((tokens, width), lambda s, c: (0, 0))
    return pl.pallas_call(
        down_kernel,
        out_shape=[jax.ShapeDtypeStruct((tokens, width), BF)] * (2 * n),
        grid_spec=pltpu.PrefetchScalarGridSpec(
            num_scalar_prefetch=1,
            grid=(slots,),
            in_specs=[
                pl.BlockSpec(info.shape, lambda s, c: (0, 0, 0)),
                act_spec,
                act_spec,
                pl.BlockSpec((1, hidden, width), lambda s, c: (s, 0, 0)),
            ],
            out_specs=[out] * (2 * n),
            scratch_shapes=[pltpu.VMEM((2 * n, slots * cap, width), F32)],
        ),
        cost_estimate=LIGHT,
        compiler_params=ROOM,
        name="down",
    )(col, info, mine, got, weight)


def add_kernel(stacked, mine_ref, *refs):
    n = (len(refs) - 1) // 2 if stacked else len(refs) // 3
    for i in range(n):
        total = (refs[i][...].astype(F32) + refs[n + i][...].astype(F32)).astype(BF)
        if stacked:
            refs[-1][i] = total
        else:
            refs[2 * n + i][...] = total


def add(mine, left, right, stacked):
    n, shape = len(left), left[0].shape
    out = jax.ShapeDtypeStruct(((n,) if stacked else ()) + shape, BF)
    return pl.pallas_call(
        functools.partial(add_kernel, stacked),
        out_shape=out if stacked else [out] * n,
        in_specs=[pl.BlockSpec(memory_space=pltpu.SMEM)]
        + [pl.BlockSpec(memory_space=pltpu.VMEM)] * (2 * n),
        cost_estimate=LIGHT,
        compiler_params=ROOM,
        name="add",
    )(mine, *left, *right)


def stack_kernel(a_ref, b_ref, out_ref):
    out_ref[0] = a_ref[...]
    out_ref[1] = b_ref[...]


def stack(a, b):
    return pl.pallas_call(
        stack_kernel,
        out_shape=jax.ShapeDtypeStruct((2,) + a.shape, a.dtype),
        cost_estimate=LIGHT,
        compiler_params=ROOM,
        name="stack",
    )(a, b)


def copy_kernel(cache_ref, out_ref):
    out_ref[...] = cache_ref[...]


def copy_cache(cache):
    pages, length, width = cache.shape
    step = 4 if pages % 4 == 0 else 1
    spec = pl.BlockSpec((step, length, width), lambda s: (s, 0, 0))
    return pl.pallas_call(
        copy_kernel,
        out_shape=jax.ShapeDtypeStruct(cache.shape, cache.dtype),
        grid=(pages // step,),
        in_specs=[spec],
        out_specs=spec,
        cost_estimate=LIGHT,
        compiler_params=ROOM,
        name="copy_cache",
    )(cache)


def page_list_kernel(dev_ref, lens_ref, pos_ref, table_ref, out_ref):
    prompts, pages_here = lens_ref.shape[0], dev_ref[1]
    dev = dev_ref[0]

    def put(found, page, base, offset, low, high, skip):
        local = page - dev * pages_here
        here = (local >= 0) & (local < pages_here)

        @pl.when(here)
        def _():
            for k, value in enumerate((local, base, offset, low, high, skip)):
                out_ref[k, found] = value

        return found + here.astype(jnp.int32)

    def prompt(q, carry):
        begin, found = carry
        length = lens_ref[q]

        def page(k, found):
            start = begin + k * PAGE
            high = jnp.minimum(length - k * PAGE, PAGE)
            base = lax.div(start, PRE_DEV)
            return put(
                found, table_ref[q, k], base, start - base * PRE_DEV, 0, high, jnp.int32(DEC_DEV)
            )

        return begin + length, lax.fori_loop(0, lax.div(length + PAGE - 1, PAGE), page, found)

    def decode(c, found):
        k = lax.div(pos_ref[c], PAGE)
        low = pos_ref[c] - k * PAGE
        base = lax.div(c, DEC_DEV)
        offset = PRE_DEV + c - base * DEC_DEV - low
        return put(found, table_ref[prompts + c, k], base, offset, low, low + 1, jnp.int32(0))

    _, found = lax.fori_loop(0, prompts, prompt, (jnp.int32(0), jnp.int32(0)))
    out_ref[6, 0] = lax.fori_loop(0, pos_ref.shape[0], decode, found)


def page_list(my_dev, pages_here, prompt_lens, decode_pos, page_table):
    smem = pl.BlockSpec(memory_space=pltpu.SMEM)
    return pl.pallas_call(
        page_list_kernel,
        out_shape=jax.ShapeDtypeStruct((8, pages_here), jnp.int32),
        in_specs=[smem] * 4,
        out_specs=smem,
        cost_estimate=LIGHT,
        compiler_params=ROOM,
        name="page_list",
    )(jnp.stack([my_dev, jnp.int32(pages_here)]), prompt_lens, decode_pos, page_table)


def page_kernel(place_ref, page_ref, *refs):
    count = len(refs) - 7
    cache_ref, out_ref, everything, held, kv_sem, in_sem, out_sem = refs[count:]
    tokens = everything.shape[1]
    length = held.shape[1]
    pages = page_ref[6, 0]
    block_copies = [
        pltpu.make_async_copy(refs[i], everything.at[place_ref[i]], kv_sem.at[i])
        for i in range(count)
    ]
    page_in = lambda k: pltpu.make_async_copy(
        cache_ref.at[page_ref[0, k]], held.at[k], in_sem.at[k]
    )
    page_out = lambda k: pltpu.make_async_copy(
        held.at[k], out_ref.at[page_ref[0, k]], out_sem.at[k]
    )
    lax.fori_loop(0, pages, lambda k, x: (page_in(k).start(), x)[1], 0)
    for copy in block_copies:
        copy.start()
    i = lax.broadcasted_iota(jnp.int32, (length, 2 * tokens), 0)
    m = lax.broadcasted_iota(jnp.int32, (length, 2 * tokens), 1)
    row = lax.broadcasted_iota(jnp.int32, (length, 1), 0)
    for copy in block_copies:
        copy.wait()

    def step(k, carry):
        base, offset = page_ref[1, k], page_ref[2, k]
        low, high, skip = page_ref[3, k], page_ref[4, k], page_ref[5, k]
        source = i + offset + jnp.where(i + offset >= PRE_DEV, skip, 0)
        select = (m == source).astype(F32).astype(BF)
        after_base = jnp.minimum(base + 1, count - 1)
        taken = jnp.dot(
            select[:, :tokens], everything[base], preferred_element_type=F32
        ) + jnp.dot(select[:, tokens:], everything[after_base], preferred_element_type=F32)
        hit = (row >= low) & (row < high)
        page_in(k).wait()
        held[k] = jnp.where(hit, taken, held[k].astype(F32)).astype(BF)
        page_out(k).start()
        return carry

    lax.fori_loop(0, pages, step, 0)
    lax.fori_loop(0, pages, lambda k, x: (page_out(k).wait(), x)[1], 0)


def write_pages(place, page_data, blocks, cache):
    pages, length, width = cache.shape
    tokens = blocks[0].shape[0]
    in_hbm = pl.BlockSpec(memory_space=pltpu.HBM)
    return pl.pallas_call(
        page_kernel,
        out_shape=jax.ShapeDtypeStruct(cache.shape, cache.dtype),
        grid_spec=pltpu.PrefetchScalarGridSpec(
            num_scalar_prefetch=2,
            grid=(),
            in_specs=[pl.BlockSpec(memory_space=pl.ANY)] * len(blocks) + [in_hbm],
            out_specs=in_hbm,
            scratch_shapes=[
                pltpu.VMEM((len(blocks), tokens, width), cache.dtype),
                pltpu.VMEM(cache.shape, cache.dtype),
                pltpu.SemaphoreType.DMA((len(blocks),)),
                pltpu.SemaphoreType.DMA((pages,)),
                pltpu.SemaphoreType.DMA((pages,)),
            ],
        ),
        input_output_aliases={2 + len(blocks): 0},
        cost_estimate=LIGHT,
        compiler_params=ROOM,
        name="write_pages",
    )(place, page_data, *blocks, cache)


def on_device_16x2(
    attn_out,
    residual,
    out_proj,
    gain_attn,
    routes,
    gate_weights,
    gate_up_w,
    down_proj,
    gain_moe,
    kv_proj,
    prompt_lens,
    decode_pos,
    page_table,
    kv_cache,
):
    rows_here, width = attn_out.shape
    my_dev = lax.axis_index("dp")
    my_col = lax.axis_index("mp")
    slots_here = gate_up_w.shape[0]
    slot_total = slots_here * NZ * NX * NC
    cap = (5 * rows_here * TOP + 4 * slot_total - 1) // (4 * slot_total)
    dot = functools.partial(jnp.dot, preferred_element_type=F32)
    own_first = lambda w: (
        lax.dynamic_slice_in_dim(w, my_col * width, width, 0),
        lax.dynamic_slice_in_dim(w, (1 - my_col) * width, width, 0),
    )

    attn_other = y_move(attn_out)
    weight = gate_up_w.transpose(2, 0, 1, 3)
    proj_own, proj_other = own_first(out_proj)
    first_half = residual.astype(F32) + dot(attn_out, proj_own)
    gates = gate_weights.T
    high = lax.reduce_precision(gates, 8, 7)
    middle = lax.reduce_precision(gates - high, 8, 7)
    padded = lambda a, lanes: jnp.pad(a, ((0, 0), (0, lanes - rows_here)))
    last = width - 2 * GATE_LANES
    names = jnp.pad(padded(routes.astype(F32).T, GATE_LANES), ((0, 0), (0, width - GATE_LANES)))
    gates = jnp.concatenate(
        [padded(high, GATE_LANES), padded(middle, GATE_LANES), padded(gates - high - middle, last)],
        axis=1,
    )
    meta = jnp.concatenate([names, gates], axis=0).astype(BF)
    weight, first_half, meta = lax.optimization_barrier((weight, first_half, meta))
    hidden = (first_half + dot(attn_other, proj_other)).astype(BF)
    hidden = lax.optimization_barrier(hidden)
    res_f = hidden.astype(F32)
    squares = jnp.sum(res_f * res_f, axis=1)
    squares = squares + y_move(squares)
    scale = lax.rsqrt(squares / D + NORM_EPS)[:, None]
    normed = (res_f * scale * gain_attn[None, :]).astype(BF)
    own = jnp.concatenate([normed, meta], axis=0)

    mine = jnp.stack([my_col, my_dev * slots_here]).astype(jnp.int32)
    infos, keeps, moving, acts, parts, sums = {}, {}, {}, {}, {}, {}

    def up_step(g, blocks, *earlier):
        send, keeps[g], infos[g] = gate_up(after(mine, *earlier), blocks, weight, cap)
        moving[g] = y_move(send)
        return keeps[g]

    def act_step(g, *earlier):
        acts[g] = activate(after(mine, *earlier), infos[g], keeps[g], moving[g])
        moving[g] = y_move(acts[g])
        return acts[g]

    def down_step(g, *earlier):
        outs = down(after(mine, *earlier), infos[g], acts[g], moving[g], down_proj)
        n = len(outs) // 2
        parts[g] = (outs[:n], [core_move(b) for b in outs[n:]])
        return outs[0]

    def sum_step(g, stacked, *earlier):
        sums[g] = add(after(mine, *earlier), *parts[g], stacked)
        return sums[g] if stacked else sums[g][-1]

    own_c = core_move(own)
    x0 = x_move(own)
    z1 = z_move(own, 1)
    z3 = z_move(own, 3)
    t = up_step(0, [own, own_c])

    columns = kv_proj.shape[1]
    proj = after(kv_proj, t)
    halves = proj.reshape(-1, columns // HD, 2, HD // 2)
    turned = jnp.stack([-halves[:, :, 1], halves[:, :, 0]], axis=2).reshape(kv_proj.shape)
    kv_own, kv_other = own_first(jnp.concatenate([proj, turned], axis=1))
    kv_own, kv_other = lax.optimization_barrier((kv_own, kv_other))

    t = act_step(0, t, kv_own, kv_other)
    x0_c = core_move(x0)
    t = up_step(1, [x0, x0_c], t)
    x13 = x_move(stack(after(z1, t), z3))
    z1_c, z3_c = core_move(z1), core_move(z3)
    z2 = z_move(z1, 1)
    t = up_step(2, [z1, z3, z1_c, z3_c], t)
    t = down_step(0, t)
    t = act_step(1, t)

    lens, positions, cache = lax.optimization_barrier((prompt_lens, decode_pos, kv_cache, t))[:3]
    pages = page_list(my_dev, kv_cache.shape[0], lens, positions, page_table)
    row_ids = my_dev * rows_here + jnp.arange(rows_here, dtype=jnp.int32)
    position, _ = row_places(row_ids, lens, positions, page_table)
    lane = jnp.arange(columns, dtype=jnp.int32)
    inverse = jnp.exp(-((lane % (HD // 2)).astype(F32) * (2.0 / HD)) * jnp.log(F32(ROPE_BASE)))
    angles = position.astype(F32)[:, None] * inverse[None, :]
    is_key = (my_col * columns + lane < KVH * HD)[None, :]
    cosine = jnp.where(is_key, jnp.cos(angles), 1.0)
    sine = jnp.where(is_key, jnp.sin(angles), 0.0)
    cache = copy_cache(cache)
    z, x, c = my_dev // (NX * NC), my_dev // NC % NX, my_dev % NC
    places = jnp.stack(
        [
            at((z + NZ - dz) % NZ, x ^ dx, c ^ dc)
            for dz in range(NZ)
            for dx in range(NX)
            for dc in range(NC)
        ]
    ).astype(jnp.int32)
    pages, cosine, sine, cache, places = lax.optimization_barrier(
        (pages, cosine, sine, cache, places)
    )

    t = sum_step(0, False, t, cosine)
    z2_c = core_move(z2)
    x2 = x_move(z2)
    t = down_step(1, t, z2)
    x1_c, x3_c = core_move(x13[0]), core_move(x13[1])
    t = up_step(3, [x13, x1_c, x3_c], t)
    t = sum_step(1, False, t)
    back_x0 = x_move(sums[1][0])
    t = act_step(2, t)
    x2_c = core_move(x2)
    t = up_step(4, [z2, x2, z2_c, x2_c], t)
    t = down_step(2, t)
    t = act_step(3, t)
    t = sum_step(2, False, t, back_x0)
    t = down_step(3, t)
    t = act_step(4, t)
    t = sum_step(3, True, t)
    back_x13 = x_move(sums[3])
    t = down_step(4, t)
    sum_step(4, False, t)
    back_x2 = x_move(sums[4][1])
    whole = lambda a, b: a.astype(F32) + b.astype(F32)
    back_1 = z_move(whole(sums[2][0], back_x13[0]).astype(BF), 3)
    back_3 = z_move(whole(sums[2][1], back_x13[1]).astype(BF), 1)
    back_2 = z_move(whole(sums[4][0], back_x2).astype(BF), 2)
    mixture = whole(sums[0][0], back_x0) + whole(back_1, back_3) + back_2.astype(F32)
    layer_out = lax.optimization_barrier((res_f + mixture).astype(BF))

    out_other = y_move(layer_out)
    gain_other = y_move(gain_moe)
    own_f, other_f = layer_out.astype(F32), out_other.astype(F32)
    out_squares = jnp.sum(own_f * own_f, axis=1) + jnp.sum(other_f * other_f, axis=1)
    scale = lax.rsqrt(out_squares / D + NORM_EPS)[:, None]
    v_own = (own_f * scale * gain_moe[None, :]).astype(BF)
    v_other = (other_f * scale * gain_other[None, :]).astype(BF)
    both = dot(v_own, kv_own) + dot(v_other, kv_other)
    rotated = (both[:, :columns] * cosine + both[:, columns:] * sine).astype(BF)

    kv = {(0, 0, 0): rotated}
    kv[1, 0, 0] = z_move(rotated, 1)
    kv[3, 0, 0] = z_move(rotated, 3)
    kv[2, 0, 0] = z_move(kv[1, 0, 0], 1)
    for dz in (0, 1, 3, 2):
        kv[dz, 1, 0] = x_move(kv[dz, 0, 0])
        for dx in range(NX):
            kv[dz, dx, 1] = core_move(kv[dz, dx, 0])
    kv_blocks = [kv[dz, dx, dc] for dz in range(NZ) for dx in range(NX) for dc in range(NC)]
    written = write_pages(places, pages, kv_blocks, cache)
    return (layer_out, written)


def solution(mesh):
    body = on_device_16x2 if (mesh.shape["dp"], mesh.shape["mp"]) == (NZ * NX * NC, 2) else on_device
    placed = (
        P("dp", "mp"),
        P("dp", "mp"),
        P(None, "mp"),
        P("mp"),
        P("dp", None),
        P("dp", None),
        P("dp", "mp", None, None),
        P("dp", None, "mp"),
        P("mp"),
        P(None, "mp"),
        P(),
        P(),
        P(),
        P("dp", None, "mp"),
    )
    return jax.shard_map(
        body,
        mesh=mesh,
        in_specs=placed,
        out_specs=(P("dp", "mp"), P("dp", None, "mp")),
        check_vma=False,
    )
```

```python
import functools
import jax
import jax.numpy as jnp
from jax import lax
from jax.experimental import pallas as pl
from jax.experimental.pallas import tpu as pltpu
from jax.sharding import PartitionSpec as P

D = 1536
TOP = 8
KVH = 8
HD = 64
PAGE = 128
PAGES_SEQ = 8
DEC_DEV = 2
ROWS_DEV = 192
PRE_DEV = 190


NORM_EPS = 1e-05
ROPE_BASE = 10000.0


def row_places(row_ids, prompt_lens, decode_pos, page_table):
    prompts = prompt_lens.shape[0]
    decodes = decode_pos.shape[0]
    device = row_ids // ROWS_DEV
    within = row_ids % ROWS_DEV
    prefill = within < PRE_DEV
    stream = device * PRE_DEV + within
    seq_ends = jnp.cumsum(prompt_lens)
    seq_pre = jnp.sum((seq_ends[None, :] <= stream[:, None]).astype(jnp.int32), axis=1)
    seq_pre = jnp.minimum(seq_pre, prompts - 1)
    seq_begin = jnp.sum(
        jnp.where(
            jnp.arange(prompts, dtype=jnp.int32)[None, :] == seq_pre[:, None],
            (seq_ends - prompt_lens)[None, :],
            0,
        ),
        axis=1,
    )
    decode_ids = device * DEC_DEV + within - PRE_DEV
    decode_at = jnp.sum(
        jnp.where(
            jnp.arange(decodes, dtype=jnp.int32)[None, :] == decode_ids[:, None],
            decode_pos[None, :],
            0,
        ),
        axis=1,
    )
    sequence = jnp.where(prefill, seq_pre, prompts + decode_ids)
    position = jnp.where(prefill, stream - seq_begin, decode_at)
    page_num = page_table.reshape(-1)[sequence * PAGES_SEQ + position // PAGE]
    return (position, page_num * PAGE + position % PAGE)


def rotate_keys(values, position, key_mask):
    half_dim = HD // 2
    inverse = jnp.exp(
        -(jnp.arange(half_dim).astype(jnp.float32) * (2.0 / HD)) * jnp.log(jnp.float32(ROPE_BASE))
    )
    angles = position[:, None] * inverse[None, :]
    cosine_table = jnp.concatenate([jnp.cos(angles), jnp.cos(angles)], axis=1)
    sine_table = jnp.concatenate([jnp.sin(angles), jnp.sin(angles)], axis=1)
    first_half = values[:, :, :half_dim]
    second_half = values[:, :, half_dim:]
    turned = jnp.concatenate([-second_half, first_half], axis=2)
    rotated = values * cosine_table[:, None, :] + turned * sine_table[:, None, :]
    return jnp.where(key_mask[None, :, None], rotated, values)


def fold_with(weight, block_in):
    return jnp.dot(block_in, weight, preferred_element_type=jnp.float32)


def on_device(
    attn_out,
    residual,
    out_proj,
    gain_attn,
    routes,
    gate_weights,
    gate_up,
    down_proj,
    gain_moe,
    kv_proj,
    prompt_lens,
    decode_pos,
    page_table,
    kv_cache,
):
    rows_here = attn_out.shape[0]
    dev_count = lax.axis_size("dp")
    my_dev = lax.axis_index("dp")
    my_col = lax.axis_index("mp")
    projected = fold_with(out_proj, lax.all_gather(attn_out, "mp", axis=1, tiled=True))
    hidden_res = lax.optimization_barrier(
        (residual.astype(jnp.float32) + projected).astype(jnp.bfloat16)
    )
    res_f = hidden_res.astype(jnp.float32)
    squares = lax.psum(jnp.sum(res_f * res_f, axis=1), "mp")
    normed = (res_f * lax.rsqrt(squares / D + NORM_EPS)[:, None] * gain_attn[None, :]).astype(
        jnp.bfloat16
    )
    slots_here = gate_up.shape[0]
    slot_total = slots_here * dev_count
    capacity = (5 * rows_here * TOP + 4 * slot_total - 1) // (4 * slot_total)
    width_here = normed.shape[1]
    flat_routes = routes.reshape(-1)
    onehot = (flat_routes[:, None] == jnp.arange(slot_total, dtype=jnp.int32)[None, :]).astype(
        jnp.int32
    )
    earlier = jnp.sum((jnp.cumsum(onehot, axis=0) - onehot) * onehot, axis=1)
    target = flat_routes * capacity + earlier
    outgoing = (
        jnp.zeros((slot_total * capacity, width_here), jnp.bfloat16)
        .at[target]
        .set(jnp.repeat(normed, TOP, axis=0))
    )
    arrived = lax.all_to_all(
        outgoing.reshape(dev_count, slots_here * capacity, width_here),
        "dp",
        split_axis=0,
        concat_axis=0,
        tiled=True,
    )
    expert_in = (
        arrived.reshape(dev_count, slots_here, capacity, width_here)
        .transpose(1, 0, 2, 3)
        .reshape(slots_here, dev_count * capacity, width_here)
    )
    partial_value = jnp.einsum(
        "srd,sdgf->srgf", expert_in, gate_up, preferred_element_type=jnp.float32
    ).astype(jnp.bfloat16)
    summed = lax.psum(partial_value, "mp").astype(jnp.float32)
    activation = (jax.nn.silu(summed[:, :, 0]) * summed[:, :, 1]).astype(jnp.bfloat16)
    expert_out = jnp.einsum(
        "srf,sfd->srd", activation, down_proj, preferred_element_type=jnp.float32
    ).astype(jnp.bfloat16)
    outbound = (
        expert_out.reshape(slots_here, dev_count, capacity, width_here)
        .transpose(1, 0, 2, 3)
        .reshape(dev_count, slots_here * capacity, width_here)
    )
    returned = lax.all_to_all(outbound, "dp", split_axis=0, concat_axis=0, tiled=True).reshape(
        slot_total * capacity, width_here
    )
    picked = returned[target].astype(jnp.float32)
    mixture = jnp.sum(
        (gate_weights.reshape(-1, 1) * picked).reshape(rows_here, TOP, width_here), axis=1
    )
    layer_out = lax.optimization_barrier((res_f + mixture).astype(jnp.bfloat16))
    out_f = layer_out.astype(jnp.float32)
    out_squares = lax.psum(jnp.sum(out_f * out_f, axis=1), "mp")
    normed_kv = (out_f * lax.rsqrt(out_squares / D + NORM_EPS)[:, None] * gain_moe[None, :]).astype(
        jnp.bfloat16
    )
    kv_local = fold_with(kv_proj, lax.all_gather(normed_kv, "mp", axis=1, tiled=True))
    heads_here = kv_proj.shape[1] // HD
    head_ids = my_col * heads_here + jnp.arange(heads_here, dtype=jnp.int32)
    row_ids = my_dev * rows_here + jnp.arange(rows_here, dtype=jnp.int32)
    position, linear = row_places(row_ids, prompt_lens, decode_pos, page_table)
    rotated = rotate_keys(
        kv_local.reshape(rows_here, heads_here, HD), position.astype(jnp.float32), head_ids < KVH
    )
    rotated = rotated.reshape(rows_here, kv_proj.shape[1]).astype(jnp.bfloat16)
    per_dev = kv_cache.shape[0] * kv_cache.shape[1]
    flat_cache = kv_cache.reshape(per_dev, kv_cache.shape[2])
    new_slots = lax.all_gather(linear, "dp", axis=0, tiled=True)
    is_mine = new_slots // per_dev == my_dev
    local_slot = jnp.where(is_mine, new_slots % per_dev, per_dev)
    written = flat_cache.at[local_slot].set(
        lax.all_gather(rotated, "dp", axis=0, tiled=True), mode="drop"
    )
    return (layer_out, written.reshape(kv_cache.shape))


NZ = 4
NX = 2
NC = 2
BF = jnp.bfloat16
F32 = jnp.float32
GATE_LANES = 256
LIGHT = pl.CostEstimate(flops=1, bytes_accessed=1, transcendentals=0)
ROOM = pltpu.CompilerParams(vmem_limit_bytes=16 << 20)


def at(z, x, c):
    return (z * NX + x) * NC + c


def moves(dz, dx, dc):
    return [
        (at(z, x, c), at((z + dz) % NZ, x ^ dx, c ^ dc))
        for z in range(NZ)
        for x in range(NX)
        for c in range(NC)
    ]


def z_move(value, dz):
    return lax.ppermute(value, "dp", moves(dz, 0, 0))


def x_move(value):
    return lax.ppermute(value, "dp", moves(0, 1, 0))


def core_move(value):
    return lax.ppermute(value, "dp", moves(0, 0, 1))


def y_move(value):
    return lax.ppermute(value, "mp", [(0, 1), (1, 0)])


def after(value, *earlier):
    return lax.optimization_barrier((value,) + earlier)[0]


def picked(info, slots, cap):
    place = lax.broadcasted_iota(jnp.int32, (cap, info.shape[1]), 0).astype(F32)
    return jnp.concatenate([(info[q : q + 1] == place).astype(F32) for q in range(slots)], axis=0)


def gate_up_kernel(count, mine_ref, w_ref, *refs):
    *sources, send_ref, keep_ref, info_ref, rows = refs
    slots, total, _ = rows.shape
    cap = total // count
    s = pl.program_id(0)

    @pl.when(s == 0)
    def _():
        blocks = [b for r in sources for b in ([r] if len(r.shape) == 2 else [r.at[0], r.at[1]])]
        tokens = info_ref.shape[2]
        r = lax.broadcasted_iota(jnp.int32, (tokens, tokens), 0)
        before = (r < lax.broadcasted_iota(jnp.int32, (tokens, tokens), 1)).astype(F32).astype(BF)
        for i, block in enumerate(blocks):
            meta = block[tokens:, :].astype(F32)
            names = meta[:TOP, :tokens]
            gates = sum(meta[TOP:, k * GATE_LANES : k * GATE_LANES + tokens] for k in range(3))
            chosen, gate = [], []
            for q in range(slots):
                same = names == (mine_ref[1] + q).astype(F32)
                chosen.append(jnp.max(same.astype(F32), axis=0, keepdims=True))
                gate.append(jnp.sum(jnp.where(same, gates, 0.0), axis=0, keepdims=True))
            unused = jnp.zeros((info_ref.shape[1] - slots, tokens), F32)
            chosen = jnp.concatenate(chosen + [unused], axis=0)
            place = jnp.dot(chosen.astype(BF), before, preferred_element_type=F32)
            place = jnp.where(chosen > 0, place, -1.0)
            rest = jnp.zeros((info_ref.shape[1] - 2 * slots, tokens), F32)
            info_ref[i] = jnp.concatenate([place[:slots]] + gate + [rest], axis=0)
            pick = picked(place, slots, cap).astype(BF)
            taken = jnp.dot(pick, block[:tokens, :], preferred_element_type=F32)
            for q in range(slots):
                rows[q, i * cap : (i + 1) * cap] = taken[q * cap : (q + 1) * cap]

    x = rows[s].astype(BF)
    half, hidden = total // 2, w_ref.shape[3]
    keeps_first = mine_ref[0] == 0
    for k in range(2):
        part = jnp.dot(x, w_ref[k, 0], preferred_element_type=F32)
        first, second = part[:half], part[half:]
        send_ref[0, :, k * hidden : (k + 1) * hidden] = jnp.where(
            keeps_first, second, first
        ).astype(BF)
        keep_ref[0, :, k * hidden : (k + 1) * hidden] = jnp.where(keeps_first, first, second)


def gate_up(mine, blocks, weight, cap):
    _, slots, width, hidden = weight.shape
    n = sum(b.ndim - 1 for b in blocks)
    tokens = blocks[0].shape[-2] - 2 * TOP
    half = n * cap // 2
    info = (n, -(-2 * slots // 8) * 8, tokens)
    out = pl.BlockSpec((1, half, 2 * hidden), lambda s, c: (s, 0, 0))
    return pl.pallas_call(
        functools.partial(gate_up_kernel, n),
        out_shape=(
            jax.ShapeDtypeStruct((slots, half, 2 * hidden), BF),
            jax.ShapeDtypeStruct((slots, half, 2 * hidden), F32),
            jax.ShapeDtypeStruct(info, F32),
        ),
        grid_spec=pltpu.PrefetchScalarGridSpec(
            num_scalar_prefetch=1,
            grid=(slots,),
            in_specs=[pl.BlockSpec((2, 1, width, hidden), lambda s, c: (0, s, 0, 0))]
            + [pl.BlockSpec(b.shape, lambda s, c, d=b.ndim: (0,) * d) for b in blocks],
            out_specs=(out, out, pl.BlockSpec(info, lambda s, c: (0, 0, 0))),
            scratch_shapes=[pltpu.VMEM((slots, n * cap, width), F32)],
        ),
        cost_estimate=LIGHT,
        compiler_params=ROOM,
        name="gate_up",
    )(mine, weight, *blocks)


def act_kernel(col_ref, info_ref, keep_ref, got_ref, act_ref):
    s = pl.program_id(0)
    slots = pl.num_programs(0)
    n = info_ref.shape[0] // 2
    cap = keep_ref.shape[1] // n
    place = lax.broadcasted_iota(jnp.int32, (cap, info_ref.shape[2]), 0).astype(F32)
    gates = []
    for i in range(n):
        block = col_ref[0] * n + i
        position = info_ref[block, pl.ds(s, 1), :]
        gate = info_ref[block, pl.ds(slots + s, 1), :]
        gates.append(jnp.sum(jnp.where(position == place, gate, 0.0), axis=1, keepdims=True))
    gate = jnp.concatenate(gates, axis=0) if n > 1 else gates[0]
    total = keep_ref[0] + got_ref[0].astype(F32)
    half = total.shape[1] // 2
    act_ref[0] = (jax.nn.silu(total[:, :half]) * total[:, half:] * gate).astype(BF)


def activate(col, info, keep, got):
    slots, rows, hidden2 = keep.shape
    spec = lambda w: pl.BlockSpec((1, rows, w), lambda s, c: (s, 0, 0))
    return pl.pallas_call(
        act_kernel,
        out_shape=jax.ShapeDtypeStruct((slots, rows, hidden2 // 2), BF),
        grid_spec=pltpu.PrefetchScalarGridSpec(
            num_scalar_prefetch=1,
            grid=(slots,),
            in_specs=[
                pl.BlockSpec(info.shape, lambda s, c: (0, 0, 0)),
                spec(hidden2),
                spec(hidden2),
            ],
            out_specs=spec(hidden2 // 2),
        ),
        cost_estimate=LIGHT,
        compiler_params=ROOM,
        name="activate",
    )(col, info, keep, got)


def down_kernel(col_ref, info_ref, mine_ref, got_ref, w_ref, *refs):
    *outs, rows = refs
    s = pl.program_id(0)
    n = len(outs) // 2
    slots = pl.num_programs(0)
    total = rows.shape[1]
    count = info_ref.shape[0]
    cap = mine_ref.shape[1] // n
    keeps_first = col_ref[0] == 0
    mine, got = mine_ref[0], got_ref[0]
    for half, act in enumerate(
        (jnp.where(keeps_first, mine, got), jnp.where(keeps_first, got, mine))
    ):
        done = jnp.dot(act, w_ref[0], preferred_element_type=F32)
        for i in range(n):
            rows[half * n + i, pl.ds(pl.multiple_of(s * cap, 8), cap), :] = done[
                i * cap : (i + 1) * cap
            ]

    @pl.when(s == slots - 1)
    def _():
        for i in range(count):
            pick = picked(info_ref[i], total // cap, cap)
            summed = jnp.dot(pick.T.astype(BF), rows[i].astype(BF), preferred_element_type=F32)
            outs[i][...] = summed.astype(BF)


def down(col, info, mine, got, weight):
    slots, half_rows, hidden = mine.shape
    n = info.shape[0] // 2
    cap = half_rows // n
    tokens, width = info.shape[2], weight.shape[2]
    act_spec = pl.BlockSpec((1, half_rows, hidden), lambda s, c: (s, 0, 0))
    out = pl.BlockSpec((tokens, width), lambda s, c: (0, 0))
    return pl.pallas_call(
        down_kernel,
        out_shape=[jax.ShapeDtypeStruct((tokens, width), BF)] * (2 * n),
        grid_spec=pltpu.PrefetchScalarGridSpec(
            num_scalar_prefetch=1,
            grid=(slots,),
            in_specs=[
                pl.BlockSpec(info.shape, lambda s, c: (0, 0, 0)),
                act_spec,
                act_spec,
                pl.BlockSpec((1, hidden, width), lambda s, c: (s, 0, 0)),
            ],
            out_specs=[out] * (2 * n),
            scratch_shapes=[pltpu.VMEM((2 * n, slots * cap, width), F32)],
        ),
        cost_estimate=LIGHT,
        compiler_params=ROOM,
        name="down",
    )(col, info, mine, got, weight)


def add_kernel(stacked, mine_ref, *refs):
    n = (len(refs) - 1) // 2 if stacked else len(refs) // 3
    for i in range(n):
        total = (refs[i][...].astype(F32) + refs[n + i][...].astype(F32)).astype(BF)
        if stacked:
            refs[-1][i] = total
        else:
            refs[2 * n + i][...] = total


def add(mine, left, right, stacked):
    n, shape = len(left), left[0].shape
    out = jax.ShapeDtypeStruct(((n,) if stacked else ()) + shape, BF)
    return pl.pallas_call(
        functools.partial(add_kernel, stacked),
        out_shape=out if stacked else [out] * n,
        in_specs=[pl.BlockSpec(memory_space=pltpu.SMEM)]
        + [pl.BlockSpec(memory_space=pltpu.VMEM)] * (2 * n),
        cost_estimate=LIGHT,
        compiler_params=ROOM,
        name="add",
    )(mine, *left, *right)


def stack_kernel(*refs):
    for i, ref in enumerate(refs[:-1]):
        refs[-1][i] = ref[...]


def stack(*arrays):
    return pl.pallas_call(
        stack_kernel,
        out_shape=jax.ShapeDtypeStruct((len(arrays),) + arrays[0].shape, arrays[0].dtype),
        cost_estimate=LIGHT,
        compiler_params=ROOM,
        name="stack",
    )(*arrays)


def copy_kernel(cache_ref, out_ref):
    out_ref[...] = cache_ref[...]


def copy_cache(cache):
    pages, length, width = cache.shape
    step = 4 if pages % 4 == 0 else 1
    spec = pl.BlockSpec((step, length, width), lambda s: (s, 0, 0))
    return pl.pallas_call(
        copy_kernel,
        out_shape=jax.ShapeDtypeStruct(cache.shape, cache.dtype),
        grid=(pages // step,),
        in_specs=[spec],
        out_specs=spec,
        cost_estimate=LIGHT,
        compiler_params=ROOM,
        name="copy_cache",
    )(cache)


ARRIVALS = tuple(
    (dz, dx, dc)
    for together in (((0, 0), (0, 1)), ((1, 0), (3, 0), (1, 1)), ((2, 0), (3, 1)), ((2, 1),))
    for dc in range(NC)
    for dz, dx in together
)


def page_list_kernel(mine_ref, lens_ref, pos_ref, table_ref, out_ref, position_ref):
    prompts, pages_here = lens_ref.shape[0], mine_ref[3]
    dev = mine_ref[2]
    row = lax.broadcasted_iota(jnp.int32, position_ref.shape, 0)
    stream = dev * PRE_DEV + row

    def put(found, page, base, offset, low, high, skip):
        local = page - dev * pages_here
        here = (local >= 0) & (local < pages_here)

        @pl.when(here)
        def _():
            for k, value in enumerate((local, base, offset, low, high, skip)):
                out_ref[k, found] = value

        return found + here.astype(jnp.int32)

    def prompt(q, carry):
        begin, found = carry
        length = lens_ref[q]
        position_ref[...] = jnp.where(
            stream >= begin, (stream - begin).astype(F32), position_ref[...]
        )

        def page(k, found):
            start = begin + k * PAGE
            high = jnp.minimum(length - k * PAGE, PAGE)
            base = lax.div(start, PRE_DEV)
            return put(
                found, table_ref[q, k], base, start - base * PRE_DEV, 0, high, jnp.int32(DEC_DEV)
            )

        return begin + length, lax.fori_loop(0, lax.div(length + PAGE - 1, PAGE), page, found)

    def decode(c, found):
        k = lax.div(pos_ref[c], PAGE)
        low = pos_ref[c] - k * PAGE
        base = lax.div(c, DEC_DEV)
        offset = PRE_DEV + c - base * DEC_DEV - low
        return put(found, table_ref[prompts + c, k], base, offset, low, low + 1, jnp.int32(0))

    position_ref[...] = jnp.zeros(position_ref.shape, F32)
    _, found = lax.fori_loop(0, prompts, prompt, (jnp.int32(0), jnp.int32(0)))
    out_ref[6, 0] = lax.fori_loop(0, pos_ref.shape[0], decode, found)
    for e in range(DEC_DEV):
        own = pos_ref[dev * DEC_DEV + e].astype(F32)
        position_ref[...] = jnp.where(row == PRE_DEV + e, own, position_ref[...])
    z, x, c = lax.div(dev, NX * NC), lax.rem(lax.div(dev, NC), NX), lax.rem(dev, NC)
    for k, (dz, dx, dc) in enumerate(ARRIVALS):
        other_x = 1 - x if dx else x
        other_c = 1 - c if dc else c
        out_ref[7, k] = at(lax.rem(z + NZ - dz, NZ), other_x, other_c)


def page_list(mine, pages_here, prompt_lens, decode_pos, page_table):
    smem = pl.BlockSpec(memory_space=pltpu.SMEM)
    return pl.pallas_call(
        page_list_kernel,
        out_shape=(
            jax.ShapeDtypeStruct((8, max(pages_here, NZ * NX * NC)), jnp.int32),
            jax.ShapeDtypeStruct((ROWS_DEV, 128), F32),
        ),
        in_specs=[smem] * 4,
        out_specs=(smem, pl.BlockSpec(memory_space=pltpu.VMEM)),
        cost_estimate=LIGHT,
        compiler_params=ROOM,
        name="page_list",
    )(mine, prompt_lens, decode_pos, page_table)


def turn_kernel(mine_ref, w_ref, out_ref):
    w = w_ref[...].astype(F32)
    n, half = w.shape[1], HD // 2
    lane = lax.broadcasted_iota(jnp.int32, w.shape, 1)
    second, first = pltpu.roll(w, n - half, 1), pltpu.roll(w, half, 1)
    out_ref[0, :, :n] = w_ref[...]
    out_ref[0, :, n:] = jnp.where(lane % HD < half, -second, first).astype(BF)


def turn(mine, w):
    rows, n = w.shape
    steps = 4
    return pl.pallas_call(
        turn_kernel,
        out_shape=jax.ShapeDtypeStruct((2, rows // 2, 2 * n), BF),
        grid_spec=pltpu.PrefetchScalarGridSpec(
            num_scalar_prefetch=1,
            grid=(2, steps),
            in_specs=[pl.BlockSpec((rows // 2 // steps, n), lambda h, i, m: (h * steps + i, 0))],
            out_specs=pl.BlockSpec(
                (1, rows // 2 // steps, 2 * n),
                lambda h, i, m: (h + m[0] - 2 * h * m[0], i, 0),
            ),
        ),
        cost_estimate=LIGHT,
        compiler_params=ROOM,
        name="turn",
    )(mine, w)


def kv_kernel(own_ref, other_ref, gain_ref, other_gain_ref, w_ref, cos_ref, sin_ref, out_ref):
    own, other = own_ref[...].astype(F32), other_ref[...].astype(F32)
    squares = jnp.sum(own * own, axis=1, keepdims=True) + jnp.sum(
        other * other, axis=1, keepdims=True
    )
    scale = lax.rsqrt(squares / D + NORM_EPS)
    both = jnp.dot(
        (own * scale * gain_ref[...]).astype(BF), w_ref[0], preferred_element_type=F32
    ) + jnp.dot(
        (other * scale * other_gain_ref[...]).astype(BF), w_ref[1], preferred_element_type=F32
    )
    n = out_ref.shape[1]
    out_ref[...] = (both[:, :n] * cos_ref[...] + both[:, n:] * sin_ref[...]).astype(BF)


def keys_values(own, other, gain, other_gain, w, cosine, sine):
    return pl.pallas_call(
        kv_kernel,
        out_shape=jax.ShapeDtypeStruct(cosine.shape, BF),
        cost_estimate=LIGHT,
        compiler_params=ROOM,
        name="keys_values",
    )(own, other, gain[None], other_gain[None], w, cosine, sine)


def page_kernel(page_ref, *refs):
    *sources, cache_ref, out_ref, window, held, in_sem, out_sem = refs
    blocks = [b for r in sources for b in ([r] if len(r.shape) == 2 else [r.at[i] for i in range(r.shape[0])])]
    tokens = blocks[0].shape[0]
    length = held.shape[1]
    pages = page_ref[6, 0]
    page_in = lambda k: pltpu.make_async_copy(
        cache_ref.at[page_ref[0, k]], held.at[k], in_sem.at[k]
    )
    page_out = lambda k: pltpu.make_async_copy(
        held.at[k], out_ref.at[page_ref[0, k]], out_sem.at[k]
    )
    lax.fori_loop(0, pages, lambda k, x: (page_in(k).start(), x)[1], 0)
    i = lax.broadcasted_iota(jnp.int32, (length, 2 * tokens), 0)
    m = lax.broadcasted_iota(jnp.int32, (length, 2 * tokens), 1)
    row = lax.broadcasted_iota(jnp.int32, (length, 1), 0)

    def step(k, carry):
        base, offset = page_ref[1, k], page_ref[2, k]
        low, high, skip = page_ref[3, k], page_ref[4, k], page_ref[5, k]
        after_base = jnp.minimum(base + 1, len(blocks) - 1)
        for b, block in enumerate(blocks):

            @pl.when(page_ref[7, b] == base)
            def _():
                window[:tokens] = block[...]

            @pl.when(page_ref[7, b] == after_base)
            def _():
                window[tokens:] = block[...]

        source = i + offset + jnp.where(i + offset >= PRE_DEV, skip, 0)
        select = (m == source).astype(F32).astype(BF)
        taken = jnp.dot(select, window[...], preferred_element_type=F32)
        hit = (row >= low) & (row < high)
        page_in(k).wait()
        held[k] = jnp.where(hit, taken, held[k].astype(F32)).astype(BF)
        page_out(k).start()
        return carry

    lax.fori_loop(0, pages, step, 0)
    lax.fori_loop(0, pages, lambda k, x: (page_out(k).wait(), x)[1], 0)


def write_pages(page_data, blocks, cache):
    pages, length, width = cache.shape
    tokens = blocks[0].shape[-2]
    in_hbm = pl.BlockSpec(memory_space=pltpu.HBM)
    return pl.pallas_call(
        page_kernel,
        out_shape=jax.ShapeDtypeStruct(cache.shape, cache.dtype),
        grid_spec=pltpu.PrefetchScalarGridSpec(
            num_scalar_prefetch=1,
            grid=(),
            in_specs=[pl.BlockSpec(memory_space=pltpu.VMEM)] * len(blocks) + [in_hbm],
            out_specs=in_hbm,
            scratch_shapes=[
                pltpu.VMEM((2 * tokens, width), cache.dtype),
                pltpu.VMEM(cache.shape, cache.dtype),
                pltpu.SemaphoreType.DMA((pages,)),
                pltpu.SemaphoreType.DMA((pages,)),
            ],
        ),
        input_output_aliases={1 + len(blocks): 0},
        cost_estimate=LIGHT,
        compiler_params=ROOM,
        name="write_pages",
    )(page_data, *blocks, cache)


def on_device_16x2(
    attn_out,
    residual,
    out_proj,
    gain_attn,
    routes,
    gate_weights,
    gate_up_w,
    down_proj,
    gain_moe,
    kv_proj,
    prompt_lens,
    decode_pos,
    page_table,
    kv_cache,
):
    rows_here, width = attn_out.shape
    my_dev = lax.axis_index("dp")
    my_col = lax.axis_index("mp")
    slots_here = gate_up_w.shape[0]
    slot_total = slots_here * NZ * NX * NC
    cap = (5 * rows_here * TOP + 4 * slot_total - 1) // (4 * slot_total)
    dot = functools.partial(jnp.dot, preferred_element_type=F32)
    own_first = lambda w: (
        lax.dynamic_slice_in_dim(w, my_col * width, width, 0),
        lax.dynamic_slice_in_dim(w, (1 - my_col) * width, width, 0),
    )

    attn_other = y_move(attn_out)
    mine = jnp.stack([my_col, my_dev * slots_here, my_dev, jnp.int32(kv_cache.shape[0])])
    table = jnp.maximum(page_table, 0)
    mine, table = lax.optimization_barrier((mine.astype(jnp.int32), table))
    proj_own, proj_other = own_first(out_proj)
    first_half = residual.astype(F32) + dot(attn_out, proj_own)
    gates = gate_weights.T
    high = lax.reduce_precision(gates, 8, 7)
    middle = lax.reduce_precision(gates - high, 8, 7)
    padded = lambda a, lanes: jnp.pad(a, ((0, 0), (0, lanes - rows_here)))
    last = width - 2 * GATE_LANES
    names = jnp.pad(padded(routes.astype(F32).T, GATE_LANES), ((0, 0), (0, width - GATE_LANES)))
    gates = jnp.concatenate(
        [padded(high, GATE_LANES), padded(middle, GATE_LANES), padded(gates - high - middle, last)],
        axis=1,
    )
    meta = jnp.concatenate([names, gates], axis=0).astype(BF)
    first_half, meta, attn_other = lax.optimization_barrier((first_half, meta, attn_other))
    hidden = (first_half + dot(attn_other, proj_other)).astype(BF)
    hidden = lax.optimization_barrier(hidden)
    res_f = hidden.astype(F32)
    squares = jnp.sum(res_f * res_f, axis=1)
    squares = squares + y_move(squares)
    scale = lax.rsqrt(squares / D + NORM_EPS)[:, None]
    normed = (res_f * scale * gain_attn[None, :]).astype(BF)
    own = jnp.concatenate([normed, meta], axis=0)

    infos, keeps, moving, acts, parts, sums = {}, {}, {}, {}, {}, {}

    def up_step(g, blocks, *earlier):
        send, keeps[g], infos[g] = gate_up(after(mine, *earlier), blocks, weight, cap)
        moving[g] = y_move(send)
        return keeps[g]

    def act_step(g, *earlier):
        acts[g] = activate(after(mine, *earlier), infos[g], keeps[g], moving[g])
        moving[g] = y_move(acts[g])
        return acts[g]

    def down_step(g, *earlier):
        outs = down(after(mine, *earlier), infos[g], acts[g], moving[g], down_proj)
        n = len(outs) // 2
        parts[g] = (outs[:n], [core_move(b) for b in outs[n:]])
        return outs[0]

    def sum_step(g, stacked, *earlier):
        sums[g] = add(after(mine, *earlier), *parts[g], stacked)
        return sums[g] if stacked else sums[g][-1]

    own_c = core_move(own)
    x0 = x_move(own)
    z1 = z_move(own, 1)
    z3 = z_move(own, 3)
    weight = after(gate_up_w, own).transpose(2, 0, 1, 3)
    x0, z1 = lax.optimization_barrier((x0, z1))
    x0_c = core_move(x0)
    x1 = x_move(z1)
    z1_c = core_move(z1)
    z2 = z_move(z1, 1)
    t = up_step(0, [own, x0, own_c, x0_c])

    columns = kv_proj.shape[1]
    kv_w = turn(after(mine, t), kv_proj)
    pages, position = page_list(
        after(mine, kv_w), kv_cache.shape[0], prompt_lens, decode_pos, table
    )
    lane = jnp.arange(columns, dtype=jnp.int32)
    inverse = jnp.exp(-((lane % (HD // 2)).astype(F32) * (2.0 / HD)) * jnp.log(F32(ROPE_BASE)))
    angles = position[:, :1] * inverse[None, :]
    is_key = (my_col * columns + lane < KVH * HD)[None, :]
    cosine = jnp.where(is_key, jnp.cos(angles), 1.0)
    sine = jnp.where(is_key, jnp.sin(angles), 0.0)
    kv_w, pages, cosine, sine = lax.optimization_barrier((kv_w, pages, cosine, sine))

    x1_c = core_move(x1)
    t = up_step(1, [z1, x1, z1_c, x1_c], t, cosine)
    z2 = after(z2, t)
    x2 = x_move(z2)
    z2_c = core_move(z2)
    t = act_step(0, t)
    cache = copy_cache(after(kv_cache, t))
    x2_c = core_move(after(x2, cache))
    t = up_step(2, [z2, x2, z2_c, x2_c], t, cache)
    x3 = x_move(after(z3, x2))
    t = act_step(1, t)
    t = down_step(0, t)
    z3_c = core_move(after(z3, t))
    x3_c = core_move(after(x3, t))
    t = up_step(3, [z3, x3, z3_c, x3_c], t)
    t = sum_step(0, False, t)
    back_x0 = x_move(t)
    t = down_step(1, t)
    t = act_step(2, t)
    t = sum_step(1, False, t)
    back_x1 = x_move(t)
    t = down_step(2, t, back_x0)
    (t,) = add(after(mine, t), sums[1][:1], [back_x1], False)
    back_1 = z_move(t, 3)
    t = act_step(3, t)
    t = sum_step(2, False, t)
    back_x2 = x_move(t)
    t = down_step(3, t, back_1)
    (t,) = add(after(mine, t), sums[2][:1], [back_x2], False)
    back_2 = z_move(t, 2)
    t = sum_step(3, False, t)
    back_x3 = x_move(t)
    (t,) = add(after(mine, t), sums[3][:1], [back_x3], False)
    back_3 = z_move(t, 1)
    whole = lambda a, b: a.astype(F32) + b.astype(F32)
    mixture = whole(sums[0][0], back_x0) + whole(back_1, back_3) + back_2.astype(F32)
    layer_out = lax.optimization_barrier((res_f + mixture).astype(BF))

    gain_other = y_move(after(gain_moe, sums[2][0]))
    rotated = keys_values(
        layer_out, y_move(layer_out), gain_moe, gain_other, kv_w, cosine, sine
    )

    x0 = x_move(rotated)
    z1 = z_move(rotated, 1)
    z3 = z_move(rotated, 3)
    x1 = x_move(after(z1, x0))
    z2 = z_move(z1, 1)
    x3 = x_move(z3)
    x2 = x_move(after(z2, x1))
    kv_blocks = []
    for together in ((rotated, x0), (z1, z3, x1), (z2, x3), (x2,)):
        block = stack(*together) if len(together) > 1 else together[0]
        kv_blocks += [block, core_move(block)]
    written = write_pages(pages, kv_blocks, cache)
    return (layer_out, written)


def solution(mesh):
    body = on_device_16x2 if (mesh.shape["dp"], mesh.shape["mp"]) == (NZ * NX * NC, 2) else on_device
    placed = (
        P("dp", "mp"),
        P("dp", "mp"),
        P(None, "mp"),
        P("mp"),
        P("dp", None),
        P("dp", None),
        P("dp", "mp", None, None),
        P("dp", None, "mp"),
        P("mp"),
        P(None, "mp"),
        P(),
        P(),
        P(),
        P("dp", None, "mp"),
    )
    return jax.shard_map(
        body,
        mesh=mesh,
        in_specs=placed,
        out_specs=(P("dp", "mp"), P("dp", None, "mp")),
        check_vma=False,
    )
```

```python
import functools
import jax
import jax.numpy as jnp
from jax import lax
from jax.experimental import pallas as pl
from jax.experimental.pallas import tpu as pltpu
from jax.sharding import PartitionSpec as P

D = 1536
TOP = 8
KVH = 8
HD = 64
PAGE = 128
PAGES_SEQ = 8
DEC_DEV = 2
ROWS_DEV = 192
PRE_DEV = 190


NORM_EPS = 1e-05
ROPE_BASE = 10000.0


def row_places(row_ids, prompt_lens, decode_pos, page_table):
    prompts = prompt_lens.shape[0]
    decodes = decode_pos.shape[0]
    device = row_ids // ROWS_DEV
    within = row_ids % ROWS_DEV
    prefill = within < PRE_DEV
    stream = device * PRE_DEV + within
    seq_ends = jnp.cumsum(prompt_lens)
    seq_pre = jnp.sum((seq_ends[None, :] <= stream[:, None]).astype(jnp.int32), axis=1)
    seq_pre = jnp.minimum(seq_pre, prompts - 1)
    seq_begin = jnp.sum(
        jnp.where(
            jnp.arange(prompts, dtype=jnp.int32)[None, :] == seq_pre[:, None],
            (seq_ends - prompt_lens)[None, :],
            0,
        ),
        axis=1,
    )
    decode_ids = device * DEC_DEV + within - PRE_DEV
    decode_at = jnp.sum(
        jnp.where(
            jnp.arange(decodes, dtype=jnp.int32)[None, :] == decode_ids[:, None],
            decode_pos[None, :],
            0,
        ),
        axis=1,
    )
    sequence = jnp.where(prefill, seq_pre, prompts + decode_ids)
    position = jnp.where(prefill, stream - seq_begin, decode_at)
    page_num = page_table.reshape(-1)[sequence * PAGES_SEQ + position // PAGE]
    return (position, page_num * PAGE + position % PAGE)


def rotate_keys(values, position, key_mask):
    half_dim = HD // 2
    inverse = jnp.exp(
        -(jnp.arange(half_dim).astype(jnp.float32) * (2.0 / HD)) * jnp.log(jnp.float32(ROPE_BASE))
    )
    angles = position[:, None] * inverse[None, :]
    cosine_table = jnp.concatenate([jnp.cos(angles), jnp.cos(angles)], axis=1)
    sine_table = jnp.concatenate([jnp.sin(angles), jnp.sin(angles)], axis=1)
    first_half = values[:, :, :half_dim]
    second_half = values[:, :, half_dim:]
    turned = jnp.concatenate([-second_half, first_half], axis=2)
    rotated = values * cosine_table[:, None, :] + turned * sine_table[:, None, :]
    return jnp.where(key_mask[None, :, None], rotated, values)


def fold_with(weight, block_in):
    return jnp.dot(block_in, weight, preferred_element_type=jnp.float32)


def on_device(
    attn_out,
    residual,
    out_proj,
    gain_attn,
    routes,
    gate_weights,
    gate_up,
    down_proj,
    gain_moe,
    kv_proj,
    prompt_lens,
    decode_pos,
    page_table,
    kv_cache,
):
    rows_here = attn_out.shape[0]
    dev_count = lax.axis_size("dp")
    my_dev = lax.axis_index("dp")
    my_col = lax.axis_index("mp")
    projected = fold_with(out_proj, lax.all_gather(attn_out, "mp", axis=1, tiled=True))
    hidden_res = lax.optimization_barrier(
        (residual.astype(jnp.float32) + projected).astype(jnp.bfloat16)
    )
    res_f = hidden_res.astype(jnp.float32)
    squares = lax.psum(jnp.sum(res_f * res_f, axis=1), "mp")
    normed = (res_f * lax.rsqrt(squares / D + NORM_EPS)[:, None] * gain_attn[None, :]).astype(
        jnp.bfloat16
    )
    slots_here = gate_up.shape[0]
    slot_total = slots_here * dev_count
    capacity = (5 * rows_here * TOP + 4 * slot_total - 1) // (4 * slot_total)
    width_here = normed.shape[1]
    flat_routes = routes.reshape(-1)
    onehot = (flat_routes[:, None] == jnp.arange(slot_total, dtype=jnp.int32)[None, :]).astype(
        jnp.int32
    )
    earlier = jnp.sum((jnp.cumsum(onehot, axis=0) - onehot) * onehot, axis=1)
    target = flat_routes * capacity + earlier
    outgoing = (
        jnp.zeros((slot_total * capacity, width_here), jnp.bfloat16)
        .at[target]
        .set(jnp.repeat(normed, TOP, axis=0))
    )
    arrived = lax.all_to_all(
        outgoing.reshape(dev_count, slots_here * capacity, width_here),
        "dp",
        split_axis=0,
        concat_axis=0,
        tiled=True,
    )
    expert_in = (
        arrived.reshape(dev_count, slots_here, capacity, width_here)
        .transpose(1, 0, 2, 3)
        .reshape(slots_here, dev_count * capacity, width_here)
    )
    partial_value = jnp.einsum(
        "srd,sdgf->srgf", expert_in, gate_up, preferred_element_type=jnp.float32
    ).astype(jnp.bfloat16)
    summed = lax.psum(partial_value, "mp").astype(jnp.float32)
    activation = (jax.nn.silu(summed[:, :, 0]) * summed[:, :, 1]).astype(jnp.bfloat16)
    expert_out = jnp.einsum(
        "srf,sfd->srd", activation, down_proj, preferred_element_type=jnp.float32
    ).astype(jnp.bfloat16)
    outbound = (
        expert_out.reshape(slots_here, dev_count, capacity, width_here)
        .transpose(1, 0, 2, 3)
        .reshape(dev_count, slots_here * capacity, width_here)
    )
    returned = lax.all_to_all(outbound, "dp", split_axis=0, concat_axis=0, tiled=True).reshape(
        slot_total * capacity, width_here
    )
    picked = returned[target].astype(jnp.float32)
    mixture = jnp.sum(
        (gate_weights.reshape(-1, 1) * picked).reshape(rows_here, TOP, width_here), axis=1
    )
    layer_out = lax.optimization_barrier((res_f + mixture).astype(jnp.bfloat16))
    out_f = layer_out.astype(jnp.float32)
    out_squares = lax.psum(jnp.sum(out_f * out_f, axis=1), "mp")
    normed_kv = (out_f * lax.rsqrt(out_squares / D + NORM_EPS)[:, None] * gain_moe[None, :]).astype(
        jnp.bfloat16
    )
    kv_local = fold_with(kv_proj, lax.all_gather(normed_kv, "mp", axis=1, tiled=True))
    heads_here = kv_proj.shape[1] // HD
    head_ids = my_col * heads_here + jnp.arange(heads_here, dtype=jnp.int32)
    row_ids = my_dev * rows_here + jnp.arange(rows_here, dtype=jnp.int32)
    position, linear = row_places(row_ids, prompt_lens, decode_pos, page_table)
    rotated = rotate_keys(
        kv_local.reshape(rows_here, heads_here, HD), position.astype(jnp.float32), head_ids < KVH
    )
    rotated = rotated.reshape(rows_here, kv_proj.shape[1]).astype(jnp.bfloat16)
    per_dev = kv_cache.shape[0] * kv_cache.shape[1]
    flat_cache = kv_cache.reshape(per_dev, kv_cache.shape[2])
    new_slots = lax.all_gather(linear, "dp", axis=0, tiled=True)
    is_mine = new_slots // per_dev == my_dev
    local_slot = jnp.where(is_mine, new_slots % per_dev, per_dev)
    written = flat_cache.at[local_slot].set(
        lax.all_gather(rotated, "dp", axis=0, tiled=True), mode="drop"
    )
    return (layer_out, written.reshape(kv_cache.shape))


NZ = 4
NX = 2
NC = 2
BF = jnp.bfloat16
F32 = jnp.float32
GATE_LANES = 256
LIGHT = pl.CostEstimate(flops=1, bytes_accessed=1, transcendentals=0)
ROOM = pltpu.CompilerParams(vmem_limit_bytes=16 << 20)


def at(z, x, c):
    return (z * NX + x) * NC + c


def moves(dz, dx, dc):
    return [
        (at(z, x, c), at((z + dz) % NZ, x ^ dx, c ^ dc))
        for z in range(NZ)
        for x in range(NX)
        for c in range(NC)
    ]


def z_move(value, dz):
    return lax.ppermute(value, "dp", moves(dz, 0, 0))


def x_move(value):
    return lax.ppermute(value, "dp", moves(0, 1, 0))


def core_move(value):
    return lax.ppermute(value, "dp", moves(0, 0, 1))


def y_move(value):
    return lax.ppermute(value, "mp", [(0, 1), (1, 0)])


def after(value, *earlier):
    return lax.optimization_barrier((value,) + earlier)[0]


def picked(info, slots, cap):
    place = lax.broadcasted_iota(jnp.int32, (cap, info.shape[1]), 0).astype(F32)
    return jnp.concatenate([(info[q : q + 1] == place).astype(F32) for q in range(slots)], axis=0)


def gate_up_kernel(count, mine_ref, w_ref, *refs):
    *sources, send_ref, keep_ref, info_ref, rows = refs
    slots, total, _ = rows.shape
    cap = total // count
    s = pl.program_id(0)

    @pl.when(s == 0)
    def _():
        blocks = [b for r in sources for b in ([r] if len(r.shape) == 2 else [r.at[0], r.at[1]])]
        tokens = info_ref.shape[2]
        r = lax.broadcasted_iota(jnp.int32, (tokens, tokens), 0)
        before = (r < lax.broadcasted_iota(jnp.int32, (tokens, tokens), 1)).astype(F32).astype(BF)
        for i, block in enumerate(blocks):
            meta = block[tokens:, :].astype(F32)
            names = meta[:TOP, :tokens]
            gates = sum(meta[TOP:, k * GATE_LANES : k * GATE_LANES + tokens] for k in range(3))
            chosen, gate = [], []
            for q in range(slots):
                same = names == (mine_ref[1] + q).astype(F32)
                chosen.append(jnp.max(same.astype(F32), axis=0, keepdims=True))
                gate.append(jnp.sum(jnp.where(same, gates, 0.0), axis=0, keepdims=True))
            unused = jnp.zeros((info_ref.shape[1] - slots, tokens), F32)
            chosen = jnp.concatenate(chosen + [unused], axis=0)
            place = jnp.dot(chosen.astype(BF), before, preferred_element_type=F32)
            place = jnp.where(chosen > 0, place, -1.0)
            rest = jnp.zeros((info_ref.shape[1] - 2 * slots, tokens), F32)
            info_ref[i] = jnp.concatenate([place[:slots]] + gate + [rest], axis=0)
            pick = picked(place, slots, cap).astype(BF)
            taken = jnp.dot(pick, block[:tokens, :], preferred_element_type=F32)
            for q in range(slots):
                rows[q, i * cap : (i + 1) * cap] = taken[q * cap : (q + 1) * cap]

    x = rows[s].astype(BF)
    half, hidden = total // 2, w_ref.shape[3]
    keeps_first = mine_ref[0] == 0
    for k in range(2):
        part = jnp.dot(x, w_ref[k, 0], preferred_element_type=F32)
        first, second = part[:half], part[half:]
        send_ref[0, :, k * hidden : (k + 1) * hidden] = jnp.where(
            keeps_first, second, first
        ).astype(BF)
        keep_ref[0, :, k * hidden : (k + 1) * hidden] = jnp.where(keeps_first, first, second)


def gate_up(mine, blocks, weight, cap):
    _, slots, width, hidden = weight.shape
    n = sum(b.ndim - 1 for b in blocks)
    tokens = blocks[0].shape[-2] - 2 * TOP
    half = n * cap // 2
    info = (n, -(-2 * slots // 8) * 8, tokens)
    out = pl.BlockSpec((1, half, 2 * hidden), lambda s, c: (s, 0, 0))
    return pl.pallas_call(
        functools.partial(gate_up_kernel, n),
        out_shape=(
            jax.ShapeDtypeStruct((slots, half, 2 * hidden), BF),
            jax.ShapeDtypeStruct((slots, half, 2 * hidden), F32),
            jax.ShapeDtypeStruct(info, F32),
        ),
        grid_spec=pltpu.PrefetchScalarGridSpec(
            num_scalar_prefetch=1,
            grid=(slots,),
            in_specs=[pl.BlockSpec((2, 1, width, hidden), lambda s, c: (0, s, 0, 0))]
            + [pl.BlockSpec(b.shape, lambda s, c, d=b.ndim: (0,) * d) for b in blocks],
            out_specs=(out, out, pl.BlockSpec(info, lambda s, c: (0, 0, 0))),
            scratch_shapes=[pltpu.VMEM((slots, n * cap, width), F32)],
        ),
        cost_estimate=LIGHT,
        compiler_params=ROOM,
        name="gate_up",
    )(mine, weight, *blocks)


def act_kernel(col_ref, info_ref, keep_ref, got_ref, act_ref):
    s = pl.program_id(0)
    slots = pl.num_programs(0)
    n = info_ref.shape[0] // 2
    cap = keep_ref.shape[1] // n
    place = lax.broadcasted_iota(jnp.int32, (cap, info_ref.shape[2]), 0).astype(F32)
    gates = []
    for i in range(n):
        block = col_ref[0] * n + i
        position = info_ref[block, pl.ds(s, 1), :]
        gate = info_ref[block, pl.ds(slots + s, 1), :]
        gates.append(jnp.sum(jnp.where(position == place, gate, 0.0), axis=1, keepdims=True))
    gate = jnp.concatenate(gates, axis=0) if n > 1 else gates[0]
    total = keep_ref[0] + got_ref[0].astype(F32)
    half = total.shape[1] // 2
    act_ref[0] = (jax.nn.silu(total[:, :half]) * total[:, half:] * gate).astype(BF)


def activate(col, info, keep, got):
    slots, rows, hidden2 = keep.shape
    spec = lambda w: pl.BlockSpec((1, rows, w), lambda s, c: (s, 0, 0))
    return pl.pallas_call(
        act_kernel,
        out_shape=jax.ShapeDtypeStruct((slots, rows, hidden2 // 2), BF),
        grid_spec=pltpu.PrefetchScalarGridSpec(
            num_scalar_prefetch=1,
            grid=(slots,),
            in_specs=[
                pl.BlockSpec(info.shape, lambda s, c: (0, 0, 0)),
                spec(hidden2),
                spec(hidden2),
            ],
            out_specs=spec(hidden2 // 2),
        ),
        cost_estimate=LIGHT,
        compiler_params=ROOM,
        name="activate",
    )(col, info, keep, got)


def down_kernel(col_ref, info_ref, mine_ref, got_ref, w_ref, *refs):
    *outs, rows = refs
    s = pl.program_id(0)
    n = len(outs) // 2
    slots = pl.num_programs(0)
    total = rows.shape[1]
    count = info_ref.shape[0]
    cap = mine_ref.shape[1] // n
    keeps_first = col_ref[0] == 0
    mine, got = mine_ref[0], got_ref[0]
    for half, act in enumerate(
        (jnp.where(keeps_first, mine, got), jnp.where(keeps_first, got, mine))
    ):
        done = jnp.dot(act, w_ref[0], preferred_element_type=F32)
        for i in range(n):
            rows[half * n + i, pl.ds(pl.multiple_of(s * cap, 8), cap), :] = done[
                i * cap : (i + 1) * cap
            ]

    @pl.when(s == slots - 1)
    def _():
        for i in range(count):
            pick = picked(info_ref[i], total // cap, cap)
            summed = jnp.dot(pick.T.astype(BF), rows[i].astype(BF), preferred_element_type=F32)
            outs[i][...] = summed.astype(BF)


def down(col, info, mine, got, weight):
    slots, half_rows, hidden = mine.shape
    n = info.shape[0] // 2
    cap = half_rows // n
    tokens, width = info.shape[2], weight.shape[2]
    act_spec = pl.BlockSpec((1, half_rows, hidden), lambda s, c: (s, 0, 0))
    out = pl.BlockSpec((tokens, width), lambda s, c: (0, 0))
    return pl.pallas_call(
        down_kernel,
        out_shape=[jax.ShapeDtypeStruct((tokens, width), BF)] * (2 * n),
        grid_spec=pltpu.PrefetchScalarGridSpec(
            num_scalar_prefetch=1,
            grid=(slots,),
            in_specs=[
                pl.BlockSpec(info.shape, lambda s, c: (0, 0, 0)),
                act_spec,
                act_spec,
                pl.BlockSpec((1, hidden, width), lambda s, c: (s, 0, 0)),
            ],
            out_specs=[out] * (2 * n),
            scratch_shapes=[pltpu.VMEM((2 * n, slots * cap, width), F32)],
        ),
        cost_estimate=LIGHT,
        compiler_params=ROOM,
        name="down",
    )(col, info, mine, got, weight)


def add_kernel(stacked, mine_ref, *refs):
    n = (len(refs) - 1) // 2 if stacked else len(refs) // 3
    for i in range(n):
        total = (refs[i][...].astype(F32) + refs[n + i][...].astype(F32)).astype(BF)
        if stacked:
            refs[-1][i] = total
        else:
            refs[2 * n + i][...] = total


def add(mine, left, right, stacked):
    n, shape = len(left), left[0].shape
    out = jax.ShapeDtypeStruct(((n,) if stacked else ()) + shape, BF)
    return pl.pallas_call(
        functools.partial(add_kernel, stacked),
        out_shape=out if stacked else [out] * n,
        in_specs=[pl.BlockSpec(memory_space=pltpu.SMEM)]
        + [pl.BlockSpec(memory_space=pltpu.VMEM)] * (2 * n),
        cost_estimate=LIGHT,
        compiler_params=ROOM,
        name="add",
    )(mine, *left, *right)


def stack_kernel(*refs):
    for i, ref in enumerate(refs[:-1]):
        refs[-1][i] = ref[...]


def stack(*arrays):
    return pl.pallas_call(
        stack_kernel,
        out_shape=jax.ShapeDtypeStruct((len(arrays),) + arrays[0].shape, arrays[0].dtype),
        cost_estimate=LIGHT,
        compiler_params=ROOM,
        name="stack",
    )(*arrays)


def copy_kernel(cache_ref, out_ref):
    out_ref[...] = cache_ref[...]


def copy_cache(cache):
    pages, length, width = cache.shape
    step = 4 if pages % 4 == 0 else 1
    spec = pl.BlockSpec((step, length, width), lambda s: (s, 0, 0))
    return pl.pallas_call(
        copy_kernel,
        out_shape=jax.ShapeDtypeStruct(cache.shape, cache.dtype),
        grid=(pages // step,),
        in_specs=[spec],
        out_specs=spec,
        cost_estimate=LIGHT,
        compiler_params=ROOM,
        name="copy_cache",
    )(cache)


ARRIVALS = tuple(
    (dz, dx, dc)
    for together in (((0, 0), (0, 1)), ((1, 0), (3, 0), (1, 1)), ((2, 0), (3, 1)), ((2, 1),))
    for dc in range(NC)
    for dz, dx in together
)


def page_list_kernel(mine_ref, lens_ref, pos_ref, table_ref, out_ref, position_ref):
    prompts, pages_here = lens_ref.shape[0], mine_ref[3]
    dev = mine_ref[2]
    row = lax.broadcasted_iota(jnp.int32, position_ref.shape, 0)
    stream = dev * PRE_DEV + row

    def put(found, page, base, offset, low, high, skip):
        local = page - dev * pages_here
        here = (local >= 0) & (local < pages_here)

        @pl.when(here)
        def _():
            for k, value in enumerate((local, base, offset, low, high, skip)):
                out_ref[k, found] = value

        return found + here.astype(jnp.int32)

    def prompt(q, carry):
        begin, found = carry
        length = lens_ref[q]
        position_ref[...] = jnp.where(
            stream >= begin, (stream - begin).astype(F32), position_ref[...]
        )

        def page(k, found):
            start = begin + k * PAGE
            high = jnp.minimum(length - k * PAGE, PAGE)
            base = lax.div(start, PRE_DEV)
            return put(
                found, table_ref[q, k], base, start - base * PRE_DEV, 0, high, jnp.int32(DEC_DEV)
            )

        return begin + length, lax.fori_loop(0, lax.div(length + PAGE - 1, PAGE), page, found)

    def decode(c, found):
        k = lax.div(pos_ref[c], PAGE)
        low = pos_ref[c] - k * PAGE
        base = lax.div(c, DEC_DEV)
        offset = PRE_DEV + c - base * DEC_DEV - low
        return put(found, table_ref[prompts + c, k], base, offset, low, low + 1, jnp.int32(0))

    position_ref[...] = jnp.zeros(position_ref.shape, F32)
    _, found = lax.fori_loop(0, prompts, prompt, (jnp.int32(0), jnp.int32(0)))
    out_ref[6, 0] = lax.fori_loop(0, pos_ref.shape[0], decode, found)
    for e in range(DEC_DEV):
        own = pos_ref[dev * DEC_DEV + e].astype(F32)
        position_ref[...] = jnp.where(row == PRE_DEV + e, own, position_ref[...])
    z, x, c = lax.div(dev, NX * NC), lax.rem(lax.div(dev, NC), NX), lax.rem(dev, NC)
    for k, (dz, dx, dc) in enumerate(ARRIVALS):
        other_x = 1 - x if dx else x
        other_c = 1 - c if dc else c
        out_ref[7, k] = at(lax.rem(z + NZ - dz, NZ), other_x, other_c)


def page_list(mine, pages_here, prompt_lens, decode_pos, page_table):
    smem = pl.BlockSpec(memory_space=pltpu.SMEM)
    return pl.pallas_call(
        page_list_kernel,
        out_shape=(
            jax.ShapeDtypeStruct((8, max(pages_here, NZ * NX * NC)), jnp.int32),
            jax.ShapeDtypeStruct((ROWS_DEV, 128), F32),
        ),
        in_specs=[smem] * 4,
        out_specs=(smem, pl.BlockSpec(memory_space=pltpu.VMEM)),
        cost_estimate=LIGHT,
        compiler_params=ROOM,
        name="page_list",
    )(mine, prompt_lens, decode_pos, page_table)


def turn_kernel(mine_ref, w_ref, out_ref):
    w = w_ref[...].astype(F32)
    n, half = w.shape[1], HD // 2
    lane = lax.broadcasted_iota(jnp.int32, w.shape, 1)
    second, first = pltpu.roll(w, n - half, 1), pltpu.roll(w, half, 1)
    out_ref[0, :, :n] = w_ref[...]
    out_ref[0, :, n:] = jnp.where(lane % HD < half, -second, first).astype(BF)


def turn(mine, w):
    rows, n = w.shape
    steps = 4
    return pl.pallas_call(
        turn_kernel,
        out_shape=jax.ShapeDtypeStruct((2, rows // 2, 2 * n), BF),
        grid_spec=pltpu.PrefetchScalarGridSpec(
            num_scalar_prefetch=1,
            grid=(2, steps),
            in_specs=[pl.BlockSpec((rows // 2 // steps, n), lambda h, i, m: (h * steps + i, 0))],
            out_specs=pl.BlockSpec(
                (1, rows // 2 // steps, 2 * n),
                lambda h, i, m: (h + m[0] - 2 * h * m[0], i, 0),
            ),
        ),
        cost_estimate=LIGHT,
        compiler_params=ROOM,
        name="turn",
    )(mine, w)


def kv_kernel(own_ref, other_ref, gain_ref, other_gain_ref, w_ref, cos_ref, sin_ref, out_ref):
    own, other = own_ref[...].astype(F32), other_ref[...].astype(F32)
    squares = jnp.sum(own * own, axis=1, keepdims=True) + jnp.sum(
        other * other, axis=1, keepdims=True
    )
    scale = lax.rsqrt(squares / D + NORM_EPS)
    both = jnp.dot(
        (own * scale * gain_ref[...]).astype(BF), w_ref[0], preferred_element_type=F32
    ) + jnp.dot(
        (other * scale * other_gain_ref[...]).astype(BF), w_ref[1], preferred_element_type=F32
    )
    n = out_ref.shape[1]
    out_ref[...] = (both[:, :n] * cos_ref[...] + both[:, n:] * sin_ref[...]).astype(BF)


def keys_values(own, other, gain, other_gain, w, cosine, sine):
    return pl.pallas_call(
        kv_kernel,
        out_shape=jax.ShapeDtypeStruct(cosine.shape, BF),
        cost_estimate=pl.CostEstimate(flops=4294967296, bytes_accessed=1, transcendentals=0),
        compiler_params=ROOM,
        name="keys_values",
    )(own, other, gain[None], other_gain[None], w, cosine, sine)


def page_kernel(page_ref, *refs):
    *sources, cache_ref, out_ref, window, held, in_sem, out_sem = refs
    blocks = [b for r in sources for b in ([r] if len(r.shape) == 2 else [r.at[i] for i in range(r.shape[0])])]
    tokens = blocks[0].shape[0]
    length = held.shape[1]
    pages = page_ref[6, 0]
    page_in = lambda k: pltpu.make_async_copy(
        cache_ref.at[page_ref[0, k]], held.at[k], in_sem.at[k]
    )
    page_out = lambda k: pltpu.make_async_copy(
        held.at[k], out_ref.at[page_ref[0, k]], out_sem.at[k]
    )
    lax.fori_loop(0, pages, lambda k, x: (page_in(k).start(), x)[1], 0)
    i = lax.broadcasted_iota(jnp.int32, (length, 2 * tokens), 0)
    m = lax.broadcasted_iota(jnp.int32, (length, 2 * tokens), 1)
    row = lax.broadcasted_iota(jnp.int32, (length, 1), 0)

    def step(k, carry):
        base, offset = page_ref[1, k], page_ref[2, k]
        low, high, skip = page_ref[3, k], page_ref[4, k], page_ref[5, k]
        after_base = jnp.minimum(base + 1, len(blocks) - 1)
        for b, block in enumerate(blocks):

            @pl.when(page_ref[7, b] == base)
            def _():
                window[:tokens] = block[...]

            @pl.when(page_ref[7, b] == after_base)
            def _():
                window[tokens:] = block[...]

        source = i + offset + jnp.where(i + offset >= PRE_DEV, skip, 0)
        select = (m == source).astype(F32).astype(BF)
        taken = jnp.dot(select, window[...], preferred_element_type=F32)
        hit = (row >= low) & (row < high)
        page_in(k).wait()
        held[k] = jnp.where(hit, taken, held[k].astype(F32)).astype(BF)
        page_out(k).start()
        return carry

    lax.fori_loop(0, pages, step, 0)
    lax.fori_loop(0, pages, lambda k, x: (page_out(k).wait(), x)[1], 0)


def write_pages(page_data, blocks, cache):
    pages, length, width = cache.shape
    tokens = blocks[0].shape[-2]
    in_hbm = pl.BlockSpec(memory_space=pltpu.HBM)
    return pl.pallas_call(
        page_kernel,
        out_shape=jax.ShapeDtypeStruct(cache.shape, cache.dtype),
        grid_spec=pltpu.PrefetchScalarGridSpec(
            num_scalar_prefetch=1,
            grid=(),
            in_specs=[pl.BlockSpec(memory_space=pltpu.VMEM)] * len(blocks) + [in_hbm],
            out_specs=in_hbm,
            scratch_shapes=[
                pltpu.VMEM((2 * tokens, width), cache.dtype),
                pltpu.VMEM(cache.shape, cache.dtype),
                pltpu.SemaphoreType.DMA((pages,)),
                pltpu.SemaphoreType.DMA((pages,)),
            ],
        ),
        input_output_aliases={1 + len(blocks): 0},
        cost_estimate=pl.CostEstimate(flops=1073741824, bytes_accessed=1, transcendentals=0),
        compiler_params=ROOM,
        name="write_pages",
    )(page_data, *blocks, cache)


ORDER = (
    ("U", 0), ("K", 0), ("B", 1), ("U", 1), ("N", 2), ("A", 0), ("Q", 2), ("C", 0), ("B", 2), ("U", 2),
    ("A", 1), ("N", 3), ("Q", 3), ("b", 3), ("D", 0), ("S", 0), ("D", 1), ("A", 2), ("U", 3), ("V", 0),
    ("S", 1), ("D", 2), ("T", 1), ("S", 2), ("A", 3), ("H", 1), ("D", 3), ("T", 2), ("S", 3), ("V", 1),
    ("T", 3),
)


def on_device_16x2(
    attn_out,
    residual,
    out_proj,
    gain_attn,
    routes,
    gate_weights,
    gate_up_w,
    down_proj,
    gain_moe,
    kv_proj,
    prompt_lens,
    decode_pos,
    page_table,
    kv_cache,
):
    rows_here, width = attn_out.shape
    my_dev = lax.axis_index("dp")
    my_col = lax.axis_index("mp")
    slots_here = gate_up_w.shape[0]
    slot_total = slots_here * NZ * NX * NC
    cap = (5 * rows_here * TOP + 4 * slot_total - 1) // (4 * slot_total)
    dot = functools.partial(jnp.dot, preferred_element_type=F32)
    own_first = lambda w: (
        lax.dynamic_slice_in_dim(w, my_col * width, width, 0),
        lax.dynamic_slice_in_dim(w, (1 - my_col) * width, width, 0),
    )

    attn_other = y_move(attn_out)
    mine = jnp.stack([my_col, my_dev * slots_here, my_dev, jnp.int32(kv_cache.shape[0])])
    table = jnp.maximum(page_table, 0)
    mine, table = lax.optimization_barrier((mine.astype(jnp.int32), table))
    proj_own, proj_other = own_first(out_proj)
    first_half = residual.astype(F32) + dot(attn_out, proj_own)
    gates = gate_weights.T
    high = lax.reduce_precision(gates, 8, 7)
    middle = lax.reduce_precision(gates - high, 8, 7)
    padded = lambda a, lanes: jnp.pad(a, ((0, 0), (0, lanes - rows_here)))
    last = width - 2 * GATE_LANES
    names = jnp.pad(padded(routes.astype(F32).T, GATE_LANES), ((0, 0), (0, width - GATE_LANES)))
    gates = jnp.concatenate(
        [padded(high, GATE_LANES), padded(middle, GATE_LANES), padded(gates - high - middle, last)],
        axis=1,
    )
    meta = jnp.concatenate([names, gates], axis=0).astype(BF)
    first_half, meta, attn_other = lax.optimization_barrier((first_half, meta, attn_other))
    hidden = (first_half + dot(attn_other, proj_other)).astype(BF)
    hidden = lax.optimization_barrier(hidden)
    res_f = hidden.astype(F32)
    squares = jnp.sum(res_f * res_f, axis=1)
    squares = squares + y_move(squares)
    scale = lax.rsqrt(squares / D + NORM_EPS)[:, None]
    normed = (res_f * scale * gain_attn[None, :]).astype(BF)
    own = jnp.concatenate([normed, meta], axis=0)

    infos, keeps, moving, acts, parts, sums = {}, {}, {}, {}, {}, {}

    def up_step(g, blocks, *earlier):
        send, keeps[g], infos[g] = gate_up(after(mine, *earlier), blocks, weight, cap)
        moving[g] = y_move(send)
        return keeps[g]

    def act_step(g, *earlier):
        acts[g] = activate(after(mine, *earlier), infos[g], keeps[g], moving[g])
        moving[g] = y_move(acts[g])
        return acts[g]

    def down_step(g, *earlier):
        outs = down(after(mine, *earlier), infos[g], acts[g], moving[g], down_proj)
        n = len(outs) // 2
        parts[g] = (outs[:n], [core_move(b) for b in outs[n:]])
        return outs[0]

    def sum_step(g, stacked, *earlier):
        sums[g] = add(after(mine, *earlier), *parts[g], stacked)
        return sums[g] if stacked else sums[g][-1]

    columns = kv_proj.shape[1]
    got = {"own": own, "own_c": core_move(own), "x0": x_move(own)}
    got["z1"], got["z3"] = z_move(own, 1), z_move(own, 3)
    weight = after(gate_up_w, own).transpose(2, 0, 1, 3)
    got["x0_c"] = core_move(got["x0"])
    got["x1"], got["z1_c"] = x_move(got["z1"]), core_move(got["z1"])
    got["z2"] = z_move(got["z1"], 1)
    groups = (("own", "x0"), ("z1", "x1"), ("z2", "x2"), ("z3", "x3"))
    t = [own]

    def up(g):
        near, far = groups[g]
        blocks = [got[k] for k in (near, far, near + "_c", far + "_c")]
        t[:] = [up_step(g, blocks, *t)]

    def act(g):
        t[:] = [act_step(g, *t)]

    def lower(g):
        t[:] = [down_step(g, *t)]

    def gather(g):
        t[:] = [sum_step(g, False, *t)]
        moving["x", g] = x_move(t[0])

    def total(g):
        whole = add(after(mine, *t), sums[g][:1], [moving["x", g]], False)
        t[:] = whole
        moving["z", g] = z_move(whole[0], (0, 3, 2, 1)[g])

    def across(g):
        got["x%d" % g] = x_move(after(got["z%d" % g], *t))

    def b_free(g):
        got["x%d_c" % g] = core_move(got["x%d" % g])

    def across_next(g):
        got["x%d" % g] = x_move(after(got["z%d" % g], got["x%d" % (g - 1)]))

    def near_core(g):
        got["z%d_c" % g] = core_move(after(got["z%d" % g], *t))

    def far_core(g):
        got["x%d_c" % g] = core_move(after(got["x%d" % g], *t))

    def tables(g):
        kv_w = turn(after(mine, *t), kv_proj)
        pages, position = page_list(
            after(mine, kv_w), kv_cache.shape[0], prompt_lens, decode_pos, table
        )
        lane = jnp.arange(columns, dtype=jnp.int32)
        inverse = jnp.exp(
            -((lane % (HD // 2)).astype(F32) * (2.0 / HD)) * jnp.log(F32(ROPE_BASE))
        )
        angles = position[:, :1] * inverse[None, :]
        is_key = (my_col * columns + lane < KVH * HD)[None, :]
        cosine = jnp.where(is_key, jnp.cos(angles), 1.0)
        sine = jnp.where(is_key, jnp.sin(angles), 0.0)
        got["tables"] = lax.optimization_barrier((kv_w, pages, cosine, sine))
        t.append(got["tables"][2])

    def cache_copy(g):
        got["cache"] = copy_cache(after(kv_cache, *t))
        t.append(got["cache"])

    def arrived(g):
        t.append(got["z%d" % g])

    def back(g):
        t.append(moving["x", g])

    def home(g):
        t.append(moving["z", g])

    steps = dict(U=up, A=act, D=lower, S=gather, T=total, X=across, N=across_next, Q=near_core, B=far_core)
    steps.update(b=b_free, K=tables, C=cache_copy, W=arrived, V=back, H=home)
    for name, g in ORDER:
        steps[name](g)
    kv_w, pages, cosine, sine = got["tables"]
    cache = got["cache"]
    whole = lambda a, b: a.astype(F32) + b.astype(F32)
    mixture = whole(sums[0][0], moving["x", 0]) + whole(moving["z", 1], moving["z", 3])
    mixture = mixture + moving["z", 2].astype(F32)
    layer_out = lax.optimization_barrier((res_f + mixture).astype(BF))

    gain_other = y_move(after(gain_moe, sums[2][0]))
    rotated = keys_values(
        layer_out, y_move(layer_out), gain_moe, gain_other, kv_w, cosine, sine
    )

    x0 = x_move(rotated)
    z1 = z_move(rotated, 1)
    z3 = z_move(rotated, 3)
    x1 = x_move(after(z1, x0))
    z2 = z_move(z1, 1)
    x3 = x_move(z3)
    x2 = x_move(after(z2, x1))
    kv_blocks = []
    for together in ((rotated, x0), (z1, z3, x1), (z2, x3), (x2,)):
        block = stack(*together) if len(together) > 1 else together[0]
        kv_blocks += [block, core_move(block)]
    written = write_pages(pages, kv_blocks, cache)
    return (layer_out, written)


def solution(mesh):
    body = on_device_16x2 if (mesh.shape["dp"], mesh.shape["mp"]) == (NZ * NX * NC, 2) else on_device
    placed = (
        P("dp", "mp"),
        P("dp", "mp"),
        P(None, "mp"),
        P("mp"),
        P("dp", None),
        P("dp", None),
        P("dp", "mp", None, None),
        P("dp", None, "mp"),
        P("mp"),
        P(None, "mp"),
        P(),
        P(),
        P(),
        P("dp", None, "mp"),
    )
    return jax.shard_map(
        body,
        mesh=mesh,
        in_specs=placed,
        out_specs=(P("dp", "mp"), P("dp", None, "mp")),
        check_vma=False,
    )
```

```python
import functools
import jax
import jax.numpy as jnp
from jax import lax
from jax.experimental import pallas as pl
from jax.experimental.pallas import tpu as pltpu
from jax.sharding import PartitionSpec as P

D = 1536
TOP = 8
KVH = 8
HD = 64
PAGE = 128
PAGES_SEQ = 8
DEC_DEV = 2
ROWS_DEV = 192
PRE_DEV = 190


NORM_EPS = 1e-05
ROPE_BASE = 10000.0


def row_places(row_ids, prompt_lens, decode_pos, page_table):
    prompts = prompt_lens.shape[0]
    decodes = decode_pos.shape[0]
    device = row_ids // ROWS_DEV
    within = row_ids % ROWS_DEV
    prefill = within < PRE_DEV
    stream = device * PRE_DEV + within
    seq_ends = jnp.cumsum(prompt_lens)
    seq_pre = jnp.sum((seq_ends[None, :] <= stream[:, None]).astype(jnp.int32), axis=1)
    seq_pre = jnp.minimum(seq_pre, prompts - 1)
    seq_begin = jnp.sum(
        jnp.where(
            jnp.arange(prompts, dtype=jnp.int32)[None, :] == seq_pre[:, None],
            (seq_ends - prompt_lens)[None, :],
            0,
        ),
        axis=1,
    )
    decode_ids = device * DEC_DEV + within - PRE_DEV
    decode_at = jnp.sum(
        jnp.where(
            jnp.arange(decodes, dtype=jnp.int32)[None, :] == decode_ids[:, None],
            decode_pos[None, :],
            0,
        ),
        axis=1,
    )
    sequence = jnp.where(prefill, seq_pre, prompts + decode_ids)
    position = jnp.where(prefill, stream - seq_begin, decode_at)
    page_num = page_table.reshape(-1)[sequence * PAGES_SEQ + position // PAGE]
    return (position, page_num * PAGE + position % PAGE)


def rotate_keys(values, position, key_mask):
    half_dim = HD // 2
    inverse = jnp.exp(
        -(jnp.arange(half_dim).astype(jnp.float32) * (2.0 / HD)) * jnp.log(jnp.float32(ROPE_BASE))
    )
    angles = position[:, None] * inverse[None, :]
    cosine_table = jnp.concatenate([jnp.cos(angles), jnp.cos(angles)], axis=1)
    sine_table = jnp.concatenate([jnp.sin(angles), jnp.sin(angles)], axis=1)
    first_half = values[:, :, :half_dim]
    second_half = values[:, :, half_dim:]
    turned = jnp.concatenate([-second_half, first_half], axis=2)
    rotated = values * cosine_table[:, None, :] + turned * sine_table[:, None, :]
    return jnp.where(key_mask[None, :, None], rotated, values)


def fold_with(weight, block_in):
    return jnp.dot(block_in, weight, preferred_element_type=jnp.float32)


def on_device(
    attn_out,
    residual,
    out_proj,
    gain_attn,
    routes,
    gate_weights,
    gate_up,
    down_proj,
    gain_moe,
    kv_proj,
    prompt_lens,
    decode_pos,
    page_table,
    kv_cache,
):
    rows_here = attn_out.shape[0]
    dev_count = lax.axis_size("dp")
    my_dev = lax.axis_index("dp")
    my_col = lax.axis_index("mp")
    projected = fold_with(out_proj, lax.all_gather(attn_out, "mp", axis=1, tiled=True))
    hidden_res = lax.optimization_barrier(
        (residual.astype(jnp.float32) + projected).astype(jnp.bfloat16)
    )
    res_f = hidden_res.astype(jnp.float32)
    squares = lax.psum(jnp.sum(res_f * res_f, axis=1), "mp")
    normed = (res_f * lax.rsqrt(squares / D + NORM_EPS)[:, None] * gain_attn[None, :]).astype(
        jnp.bfloat16
    )
    slots_here = gate_up.shape[0]
    slot_total = slots_here * dev_count
    capacity = (5 * rows_here * TOP + 4 * slot_total - 1) // (4 * slot_total)
    width_here = normed.shape[1]
    flat_routes = routes.reshape(-1)
    onehot = (flat_routes[:, None] == jnp.arange(slot_total, dtype=jnp.int32)[None, :]).astype(
        jnp.int32
    )
    earlier = jnp.sum((jnp.cumsum(onehot, axis=0) - onehot) * onehot, axis=1)
    target = flat_routes * capacity + earlier
    outgoing = (
        jnp.zeros((slot_total * capacity, width_here), jnp.bfloat16)
        .at[target]
        .set(jnp.repeat(normed, TOP, axis=0))
    )
    arrived = lax.all_to_all(
        outgoing.reshape(dev_count, slots_here * capacity, width_here),
        "dp",
        split_axis=0,
        concat_axis=0,
        tiled=True,
    )
    expert_in = (
        arrived.reshape(dev_count, slots_here, capacity, width_here)
        .transpose(1, 0, 2, 3)
        .reshape(slots_here, dev_count * capacity, width_here)
    )
    partial_value = jnp.einsum(
        "srd,sdgf->srgf", expert_in, gate_up, preferred_element_type=jnp.float32
    ).astype(jnp.bfloat16)
    summed = lax.psum(partial_value, "mp").astype(jnp.float32)
    activation = (jax.nn.silu(summed[:, :, 0]) * summed[:, :, 1]).astype(jnp.bfloat16)
    expert_out = jnp.einsum(
        "srf,sfd->srd", activation, down_proj, preferred_element_type=jnp.float32
    ).astype(jnp.bfloat16)
    outbound = (
        expert_out.reshape(slots_here, dev_count, capacity, width_here)
        .transpose(1, 0, 2, 3)
        .reshape(dev_count, slots_here * capacity, width_here)
    )
    returned = lax.all_to_all(outbound, "dp", split_axis=0, concat_axis=0, tiled=True).reshape(
        slot_total * capacity, width_here
    )
    picked = returned[target].astype(jnp.float32)
    mixture = jnp.sum(
        (gate_weights.reshape(-1, 1) * picked).reshape(rows_here, TOP, width_here), axis=1
    )
    layer_out = lax.optimization_barrier((res_f + mixture).astype(jnp.bfloat16))
    out_f = layer_out.astype(jnp.float32)
    out_squares = lax.psum(jnp.sum(out_f * out_f, axis=1), "mp")
    normed_kv = (out_f * lax.rsqrt(out_squares / D + NORM_EPS)[:, None] * gain_moe[None, :]).astype(
        jnp.bfloat16
    )
    kv_local = fold_with(kv_proj, lax.all_gather(normed_kv, "mp", axis=1, tiled=True))
    heads_here = kv_proj.shape[1] // HD
    head_ids = my_col * heads_here + jnp.arange(heads_here, dtype=jnp.int32)
    row_ids = my_dev * rows_here + jnp.arange(rows_here, dtype=jnp.int32)
    position, linear = row_places(row_ids, prompt_lens, decode_pos, page_table)
    rotated = rotate_keys(
        kv_local.reshape(rows_here, heads_here, HD), position.astype(jnp.float32), head_ids < KVH
    )
    rotated = rotated.reshape(rows_here, kv_proj.shape[1]).astype(jnp.bfloat16)
    per_dev = kv_cache.shape[0] * kv_cache.shape[1]
    flat_cache = kv_cache.reshape(per_dev, kv_cache.shape[2])
    new_slots = lax.all_gather(linear, "dp", axis=0, tiled=True)
    is_mine = new_slots // per_dev == my_dev
    local_slot = jnp.where(is_mine, new_slots % per_dev, per_dev)
    written = flat_cache.at[local_slot].set(
        lax.all_gather(rotated, "dp", axis=0, tiled=True), mode="drop"
    )
    return (layer_out, written.reshape(kv_cache.shape))


NZ = 4
NX = 2
NC = 2
BF = jnp.bfloat16
F32 = jnp.float32
GATE_LANES = 256
LIGHT = pl.CostEstimate(flops=1, bytes_accessed=1, transcendentals=0)
ROOM = pltpu.CompilerParams(vmem_limit_bytes=16 << 20)


def at(z, x, c):
    return (z * NX + x) * NC + c


def moves(dz, dx, dc):
    return [
        (at(z, x, c), at((z + dz) % NZ, x ^ dx, c ^ dc))
        for z in range(NZ)
        for x in range(NX)
        for c in range(NC)
    ]


def z_move(value, dz):
    return lax.ppermute(value, "dp", moves(dz, 0, 0))


def x_move(value):
    return lax.ppermute(value, "dp", moves(0, 1, 0))


def core_move(value):
    return lax.ppermute(value, "dp", moves(0, 0, 1))


def y_move(value):
    return lax.ppermute(value, "mp", [(0, 1), (1, 0)])


def after(value, *earlier):
    return lax.optimization_barrier((value,) + earlier)[0]


def picked(info, slots, cap):
    place = lax.broadcasted_iota(jnp.int32, (cap, info.shape[1]), 0).astype(F32)
    return jnp.concatenate([(info[q : q + 1] == place).astype(F32) for q in range(slots)], axis=0)


def gate_up_kernel(count, mine_ref, w_ref, *refs):
    *sources, send_ref, keep_ref, info_ref, rows = refs
    slots, total, _ = rows.shape
    cap = total // count
    s = pl.program_id(0)

    @pl.when(s == 0)
    def _():
        blocks = [b for r in sources for b in ([r] if len(r.shape) == 2 else [r.at[0], r.at[1]])]
        tokens = info_ref.shape[2]
        r = lax.broadcasted_iota(jnp.int32, (tokens, tokens), 0)
        before = (r < lax.broadcasted_iota(jnp.int32, (tokens, tokens), 1)).astype(F32).astype(BF)
        for i, block in enumerate(blocks):
            meta = block[tokens:, :].astype(F32)
            names = meta[:TOP, :tokens]
            gates = sum(meta[TOP:, k * GATE_LANES : k * GATE_LANES + tokens] for k in range(3))
            chosen, gate = [], []
            for q in range(slots):
                same = names == (mine_ref[1] + q).astype(F32)
                chosen.append(jnp.max(same.astype(F32), axis=0, keepdims=True))
                gate.append(jnp.sum(jnp.where(same, gates, 0.0), axis=0, keepdims=True))
            unused = jnp.zeros((info_ref.shape[1] - slots, tokens), F32)
            chosen = jnp.concatenate(chosen + [unused], axis=0)
            place = jnp.dot(chosen.astype(BF), before, preferred_element_type=F32)
            place = jnp.where(chosen > 0, place, -1.0)
            rest = jnp.zeros((info_ref.shape[1] - 2 * slots, tokens), F32)
            info_ref[i] = jnp.concatenate([place[:slots]] + gate + [rest], axis=0)
            pick = picked(place, slots, cap).astype(BF)
            taken = jnp.dot(pick, block[:tokens, :], preferred_element_type=F32)
            for q in range(slots):
                rows[q, i * cap : (i + 1) * cap] = taken[q * cap : (q + 1) * cap]

    x = rows[s].astype(BF)
    half, hidden = total // 2, w_ref.shape[3]
    keeps_first = mine_ref[0] == 0
    for k in range(2):
        part = jnp.dot(x, w_ref[k, 0], preferred_element_type=F32)
        first, second = part[:half], part[half:]
        send_ref[0, :, k * hidden : (k + 1) * hidden] = jnp.where(
            keeps_first, second, first
        ).astype(BF)
        keep_ref[0, :, k * hidden : (k + 1) * hidden] = jnp.where(keeps_first, first, second)


def gate_up(mine, blocks, weight, cap):
    _, slots, width, hidden = weight.shape
    n = sum(b.ndim - 1 for b in blocks)
    tokens = blocks[0].shape[-2] - 2 * TOP
    half = n * cap // 2
    info = (n, -(-2 * slots // 8) * 8, tokens)
    out = pl.BlockSpec((1, half, 2 * hidden), lambda s, c: (s, 0, 0))
    return pl.pallas_call(
        functools.partial(gate_up_kernel, n),
        out_shape=(
            jax.ShapeDtypeStruct((slots, half, 2 * hidden), BF),
            jax.ShapeDtypeStruct((slots, half, 2 * hidden), F32),
            jax.ShapeDtypeStruct(info, F32),
        ),
        grid_spec=pltpu.PrefetchScalarGridSpec(
            num_scalar_prefetch=1,
            grid=(slots,),
            in_specs=[pl.BlockSpec((2, 1, width, hidden), lambda s, c: (0, s, 0, 0))]
            + [pl.BlockSpec(b.shape, lambda s, c, d=b.ndim: (0,) * d) for b in blocks],
            out_specs=(out, out, pl.BlockSpec(info, lambda s, c: (0, 0, 0))),
            scratch_shapes=[pltpu.VMEM((slots, n * cap, width), F32)],
        ),
        cost_estimate=LIGHT,
        compiler_params=ROOM,
        name="gate_up",
    )(mine, weight, *blocks)


def act_kernel(col_ref, info_ref, keep_ref, got_ref, act_ref):
    s = pl.program_id(0)
    slots = pl.num_programs(0)
    n = info_ref.shape[0] // 2
    cap = keep_ref.shape[1] // n
    place = lax.broadcasted_iota(jnp.int32, (cap, info_ref.shape[2]), 0).astype(F32)
    gates = []
    for i in range(n):
        block = col_ref[0] * n + i
        position = info_ref[block, pl.ds(s, 1), :]
        gate = info_ref[block, pl.ds(slots + s, 1), :]
        gates.append(jnp.sum(jnp.where(position == place, gate, 0.0), axis=1, keepdims=True))
    gate = jnp.concatenate(gates, axis=0) if n > 1 else gates[0]
    total = keep_ref[0] + got_ref[0].astype(F32)
    half = total.shape[1] // 2
    act_ref[0] = (jax.nn.silu(total[:, :half]) * total[:, half:] * gate).astype(BF)


def activate(col, info, keep, got):
    slots, rows, hidden2 = keep.shape
    spec = lambda w: pl.BlockSpec((1, rows, w), lambda s, c: (s, 0, 0))
    return pl.pallas_call(
        act_kernel,
        out_shape=jax.ShapeDtypeStruct((slots, rows, hidden2 // 2), BF),
        grid_spec=pltpu.PrefetchScalarGridSpec(
            num_scalar_prefetch=1,
            grid=(slots,),
            in_specs=[
                pl.BlockSpec(info.shape, lambda s, c: (0, 0, 0)),
                spec(hidden2),
                spec(hidden2),
            ],
            out_specs=spec(hidden2 // 2),
        ),
        cost_estimate=LIGHT,
        compiler_params=ROOM,
        name="activate",
    )(col, info, keep, got)


def down_kernel(col_ref, info_ref, mine_ref, got_ref, w_ref, *refs):
    *outs, rows = refs
    s = pl.program_id(0)
    n = len(outs) // 2
    slots = pl.num_programs(0)
    total = rows.shape[1]
    count = info_ref.shape[0]
    cap = mine_ref.shape[1] // n
    keeps_first = col_ref[0] == 0
    mine, got = mine_ref[0], got_ref[0]
    for half, act in enumerate(
        (jnp.where(keeps_first, mine, got), jnp.where(keeps_first, got, mine))
    ):
        done = jnp.dot(act, w_ref[0], preferred_element_type=F32)
        for i in range(n):
            rows[half * n + i, pl.ds(pl.multiple_of(s * cap, 8), cap), :] = done[
                i * cap : (i + 1) * cap
            ]

    @pl.when(s == slots - 1)
    def _():
        for i in range(count):
            pick = picked(info_ref[i], total // cap, cap)
            summed = jnp.dot(pick.T.astype(BF), rows[i].astype(BF), preferred_element_type=F32)
            outs[i][...] = summed.astype(BF)


def down(col, info, mine, got, weight):
    slots, half_rows, hidden = mine.shape
    n = info.shape[0] // 2
    cap = half_rows // n
    tokens, width = info.shape[2], weight.shape[2]
    act_spec = pl.BlockSpec((1, half_rows, hidden), lambda s, c: (s, 0, 0))
    out = pl.BlockSpec((tokens, width), lambda s, c: (0, 0))
    return pl.pallas_call(
        down_kernel,
        out_shape=[jax.ShapeDtypeStruct((tokens, width), BF)] * (2 * n),
        grid_spec=pltpu.PrefetchScalarGridSpec(
            num_scalar_prefetch=1,
            grid=(slots,),
            in_specs=[
                pl.BlockSpec(info.shape, lambda s, c: (0, 0, 0)),
                act_spec,
                act_spec,
                pl.BlockSpec((1, hidden, width), lambda s, c: (s, 0, 0)),
            ],
            out_specs=[out] * (2 * n),
            scratch_shapes=[pltpu.VMEM((2 * n, slots * cap, width), F32)],
        ),
        cost_estimate=LIGHT,
        compiler_params=ROOM,
        name="down",
    )(col, info, mine, got, weight)


def add_kernel(stacked, mine_ref, *refs):
    n = (len(refs) - 1) // 2 if stacked else len(refs) // 3
    for i in range(n):
        total = (refs[i][...].astype(F32) + refs[n + i][...].astype(F32)).astype(BF)
        if stacked:
            refs[-1][i] = total
        else:
            refs[2 * n + i][...] = total


def add(mine, left, right, stacked):
    n, shape = len(left), left[0].shape
    out = jax.ShapeDtypeStruct(((n,) if stacked else ()) + shape, BF)
    return pl.pallas_call(
        functools.partial(add_kernel, stacked),
        out_shape=out if stacked else [out] * n,
        in_specs=[pl.BlockSpec(memory_space=pltpu.SMEM)]
        + [pl.BlockSpec(memory_space=pltpu.VMEM)] * (2 * n),
        cost_estimate=LIGHT,
        compiler_params=ROOM,
        name="add",
    )(mine, *left, *right)


def stack_kernel(*refs):
    for i, ref in enumerate(refs[:-1]):
        refs[-1][i] = ref[...]


def stack(*arrays):
    return pl.pallas_call(
        stack_kernel,
        out_shape=jax.ShapeDtypeStruct((len(arrays),) + arrays[0].shape, arrays[0].dtype),
        cost_estimate=LIGHT,
        compiler_params=ROOM,
        name="stack",
    )(*arrays)


def copy_kernel(cache_ref, out_ref):
    out_ref[...] = cache_ref[...]


def copy_cache(cache):
    pages, length, width = cache.shape
    step = 4 if pages % 4 == 0 else 1
    spec = pl.BlockSpec((step, length, width), lambda s: (s, 0, 0))
    return pl.pallas_call(
        copy_kernel,
        out_shape=jax.ShapeDtypeStruct(cache.shape, cache.dtype),
        grid=(pages // step,),
        in_specs=[spec],
        out_specs=spec,
        cost_estimate=LIGHT,
        compiler_params=ROOM,
        name="copy_cache",
    )(cache)


ARRIVALS = tuple(
    (dz, dx, dc)
    for together in (((0, 0), (0, 1)), ((1, 0), (3, 0), (1, 1)), ((2, 0), (3, 1)), ((2, 1),))
    for dc in range(NC)
    for dz, dx in together
)


def page_list_kernel(mine_ref, lens_ref, pos_ref, table_ref, out_ref, position_ref):
    prompts, pages_here = lens_ref.shape[0], mine_ref[3]
    dev = mine_ref[2]
    row = lax.broadcasted_iota(jnp.int32, position_ref.shape, 0)
    stream = dev * PRE_DEV + row

    def put(found, page, base, offset, low, high, skip):
        local = page - dev * pages_here
        here = (local >= 0) & (local < pages_here)

        @pl.when(here)
        def _():
            for k, value in enumerate((local, base, offset, low, high, skip)):
                out_ref[k, found] = value

        return found + here.astype(jnp.int32)

    def prompt(q, carry):
        begin, found = carry
        length = lens_ref[q]
        position_ref[...] = jnp.where(
            stream >= begin, (stream - begin).astype(F32), position_ref[...]
        )

        def page(k, found):
            start = begin + k * PAGE
            high = jnp.minimum(length - k * PAGE, PAGE)
            base = lax.div(start, PRE_DEV)
            return put(
                found, table_ref[q, k], base, start - base * PRE_DEV, 0, high, jnp.int32(DEC_DEV)
            )

        return begin + length, lax.fori_loop(0, lax.div(length + PAGE - 1, PAGE), page, found)

    def decode(c, found):
        k = lax.div(pos_ref[c], PAGE)
        low = pos_ref[c] - k * PAGE
        base = lax.div(c, DEC_DEV)
        offset = PRE_DEV + c - base * DEC_DEV - low
        return put(found, table_ref[prompts + c, k], base, offset, low, low + 1, jnp.int32(0))

    position_ref[...] = jnp.zeros(position_ref.shape, F32)
    _, found = lax.fori_loop(0, prompts, prompt, (jnp.int32(0), jnp.int32(0)))
    out_ref[6, 0] = lax.fori_loop(0, pos_ref.shape[0], decode, found)
    for e in range(DEC_DEV):
        own = pos_ref[dev * DEC_DEV + e].astype(F32)
        position_ref[...] = jnp.where(row == PRE_DEV + e, own, position_ref[...])
    z, x, c = lax.div(dev, NX * NC), lax.rem(lax.div(dev, NC), NX), lax.rem(dev, NC)
    for k, (dz, dx, dc) in enumerate(ARRIVALS):
        other_x = 1 - x if dx else x
        other_c = 1 - c if dc else c
        out_ref[7, k] = at(lax.rem(z + NZ - dz, NZ), other_x, other_c)


def page_list(mine, pages_here, prompt_lens, decode_pos, page_table):
    smem = pl.BlockSpec(memory_space=pltpu.SMEM)
    return pl.pallas_call(
        page_list_kernel,
        out_shape=(
            jax.ShapeDtypeStruct((8, max(pages_here, NZ * NX * NC)), jnp.int32),
            jax.ShapeDtypeStruct((ROWS_DEV, 128), F32),
        ),
        in_specs=[smem] * 4,
        out_specs=(smem, pl.BlockSpec(memory_space=pltpu.VMEM)),
        cost_estimate=LIGHT,
        compiler_params=ROOM,
        name="page_list",
    )(mine, prompt_lens, decode_pos, page_table)


def turn_kernel(mine_ref, w_ref, out_ref):
    w = w_ref[...].astype(F32)
    n, half = w.shape[1], HD // 2
    lane = lax.broadcasted_iota(jnp.int32, w.shape, 1)
    second, first = pltpu.roll(w, n - half, 1), pltpu.roll(w, half, 1)
    out_ref[0, :, :n] = w_ref[...]
    out_ref[0, :, n:] = jnp.where(lane % HD < half, -second, first).astype(BF)


def turn(mine, w):
    rows, n = w.shape
    steps = 4
    return pl.pallas_call(
        turn_kernel,
        out_shape=jax.ShapeDtypeStruct((2, rows // 2, 2 * n), BF),
        grid_spec=pltpu.PrefetchScalarGridSpec(
            num_scalar_prefetch=1,
            grid=(2, steps),
            in_specs=[pl.BlockSpec((rows // 2 // steps, n), lambda h, i, m: (h * steps + i, 0))],
            out_specs=pl.BlockSpec(
                (1, rows // 2 // steps, 2 * n),
                lambda h, i, m: (h + m[0] - 2 * h * m[0], i, 0),
            ),
        ),
        cost_estimate=LIGHT,
        compiler_params=ROOM,
        name="turn",
    )(mine, w)


def kv_kernel(own_ref, other_ref, gain_ref, other_gain_ref, w_ref, cos_ref, sin_ref, out_ref):
    own, other = own_ref[...].astype(F32), other_ref[...].astype(F32)
    squares = jnp.sum(own * own, axis=1, keepdims=True) + jnp.sum(
        other * other, axis=1, keepdims=True
    )
    scale = lax.rsqrt(squares / D + NORM_EPS)
    both = jnp.dot(
        (own * scale * gain_ref[...]).astype(BF), w_ref[0], preferred_element_type=F32
    ) + jnp.dot(
        (other * scale * other_gain_ref[...]).astype(BF), w_ref[1], preferred_element_type=F32
    )
    n = out_ref.shape[1]
    out_ref[...] = (both[:, :n] * cos_ref[...] + both[:, n:] * sin_ref[...]).astype(BF)


def keys_values(own, other, gain, other_gain, w, cosine, sine):
    return pl.pallas_call(
        kv_kernel,
        out_shape=jax.ShapeDtypeStruct(cosine.shape, BF),
        cost_estimate=pl.CostEstimate(flops=4294967296, bytes_accessed=1, transcendentals=0),
        compiler_params=ROOM,
        name="keys_values",
    )(own, other, gain[None], other_gain[None], w, cosine, sine)


def page_kernel(page_ref, *refs):
    *sources, cache_ref, out_ref, window, held, in_sem, out_sem = refs
    blocks = [b for r in sources for b in ([r] if len(r.shape) == 2 else [r.at[i] for i in range(r.shape[0])])]
    tokens = blocks[0].shape[0]
    length = held.shape[1]
    pages = page_ref[6, 0]
    page_in = lambda k: pltpu.make_async_copy(
        cache_ref.at[page_ref[0, k]], held.at[k], in_sem.at[k]
    )
    page_out = lambda k: pltpu.make_async_copy(
        held.at[k], out_ref.at[page_ref[0, k]], out_sem.at[k]
    )
    lax.fori_loop(0, pages, lambda k, x: (page_in(k).start(), x)[1], 0)
    i = lax.broadcasted_iota(jnp.int32, (length, 2 * tokens), 0)
    m = lax.broadcasted_iota(jnp.int32, (length, 2 * tokens), 1)
    row = lax.broadcasted_iota(jnp.int32, (length, 1), 0)

    def step(k, carry):
        base, offset = page_ref[1, k], page_ref[2, k]
        low, high, skip = page_ref[3, k], page_ref[4, k], page_ref[5, k]
        after_base = jnp.minimum(base + 1, len(blocks) - 1)
        for b, block in enumerate(blocks):

            @pl.when(page_ref[7, b] == base)
            def _():
                window[:tokens] = block[...]

            @pl.when(page_ref[7, b] == after_base)
            def _():
                window[tokens:] = block[...]

        source = i + offset + jnp.where(i + offset >= PRE_DEV, skip, 0)
        select = (m == source).astype(F32).astype(BF)
        taken = jnp.dot(select, window[...], preferred_element_type=F32)
        hit = (row >= low) & (row < high)
        page_in(k).wait()
        held[k] = jnp.where(hit, taken, held[k].astype(F32)).astype(BF)
        page_out(k).start()
        return carry

    lax.fori_loop(0, pages, step, 0)
    lax.fori_loop(0, pages, lambda k, x: (page_out(k).wait(), x)[1], 0)


def write_pages(page_data, blocks, cache):
    pages, length, width = cache.shape
    tokens = blocks[0].shape[-2]
    in_hbm = pl.BlockSpec(memory_space=pltpu.HBM)
    return pl.pallas_call(
        page_kernel,
        out_shape=jax.ShapeDtypeStruct(cache.shape, cache.dtype),
        grid_spec=pltpu.PrefetchScalarGridSpec(
            num_scalar_prefetch=1,
            grid=(),
            in_specs=[pl.BlockSpec(memory_space=pltpu.VMEM)] * len(blocks) + [in_hbm],
            out_specs=in_hbm,
            scratch_shapes=[
                pltpu.VMEM((2 * tokens, width), cache.dtype),
                pltpu.VMEM(cache.shape, cache.dtype),
                pltpu.SemaphoreType.DMA((pages,)),
                pltpu.SemaphoreType.DMA((pages,)),
            ],
        ),
        input_output_aliases={1 + len(blocks): 0},
        cost_estimate=pl.CostEstimate(flops=1073741824, bytes_accessed=1, transcendentals=0),
        compiler_params=ROOM,
        name="write_pages",
    )(page_data, *blocks, cache)


ORDER = (
    ("U", 0), ("K", 0), ("B", 1), ("U", 1), ("N", 2), ("A", 0), ("Q", 2), ("C", 0), ("B", 2), ("U", 2),
    ("A", 1), ("N", 3), ("Q", 3), ("b", 3), ("D", 0), ("S", 0), ("D", 1), ("A", 2), ("U", 3), ("V", 0),
    ("S", 1), ("D", 2), ("T", 1), ("S", 2), ("A", 3), ("H", 1), ("D", 3), ("T", 2), ("S", 3), ("V", 1),
    ("T", 3),
)


def on_device_16x2(
    attn_out,
    residual,
    out_proj,
    gain_attn,
    routes,
    gate_weights,
    gate_up_w,
    down_proj,
    gain_moe,
    kv_proj,
    prompt_lens,
    decode_pos,
    page_table,
    kv_cache,
):
    rows_here, width = attn_out.shape
    my_dev = lax.axis_index("dp")
    my_col = lax.axis_index("mp")
    slots_here = gate_up_w.shape[0]
    slot_total = slots_here * NZ * NX * NC
    cap = (5 * rows_here * TOP + 4 * slot_total - 1) // (4 * slot_total)
    dot = functools.partial(jnp.dot, preferred_element_type=F32)
    own_first = lambda w: (
        lax.dynamic_slice_in_dim(w, my_col * width, width, 0),
        lax.dynamic_slice_in_dim(w, (1 - my_col) * width, width, 0),
    )

    attn_other = y_move(attn_out)
    mine = jnp.stack([my_col, my_dev * slots_here, my_dev, jnp.int32(kv_cache.shape[0])])
    table = jnp.maximum(page_table, 0)
    mine, table = lax.optimization_barrier((mine.astype(jnp.int32), table))
    proj_own, proj_other = own_first(out_proj)
    first_half = residual.astype(F32) + dot(attn_out, proj_own)
    gates = gate_weights.T
    high = lax.reduce_precision(gates, 8, 7)
    middle = lax.reduce_precision(gates - high, 8, 7)
    padded = lambda a, lanes: jnp.pad(a, ((0, 0), (0, lanes - rows_here)))
    last = width - 2 * GATE_LANES
    names = jnp.pad(padded(routes.astype(F32).T, GATE_LANES), ((0, 0), (0, width - GATE_LANES)))
    gates = jnp.concatenate(
        [padded(high, GATE_LANES), padded(middle, GATE_LANES), padded(gates - high - middle, last)],
        axis=1,
    )
    meta = jnp.concatenate([names, gates], axis=0).astype(BF)
    first_half, meta, attn_other, gain_other = lax.optimization_barrier(
        (first_half, meta, attn_other, y_move(gain_moe))
    )
    hidden = (first_half + dot(attn_other, proj_other)).astype(BF)
    hidden = lax.optimization_barrier(hidden)
    res_f = hidden.astype(F32)
    squares = jnp.sum(res_f * res_f, axis=1)
    squares = squares + y_move(squares)
    scale = lax.rsqrt(squares / D + NORM_EPS)[:, None]
    normed = (res_f * scale * gain_attn[None, :]).astype(BF)
    own = jnp.concatenate([normed, meta], axis=0)

    infos, keeps, moving, acts, parts, sums = {}, {}, {}, {}, {}, {}

    def up_step(g, blocks, *earlier):
        send, keeps[g], infos[g] = gate_up(after(mine, *earlier), blocks, weight, cap)
        moving[g] = y_move(send)
        return keeps[g]

    def act_step(g, *earlier):
        acts[g] = activate(after(mine, *earlier), infos[g], keeps[g], moving[g])
        moving[g] = y_move(acts[g])
        return acts[g]

    def down_step(g, *earlier):
        outs = down(after(mine, *earlier), infos[g], acts[g], moving[g], down_proj)
        n = len(outs) // 2
        parts[g] = (outs[:n], [core_move(b) for b in outs[n:]])
        return outs[0]

    def sum_step(g, stacked, *earlier):
        sums[g] = add(after(mine, *earlier), *parts[g], stacked)
        return sums[g] if stacked else sums[g][-1]

    columns = kv_proj.shape[1]
    got = {"own": own, "own_c": core_move(own), "x0": x_move(own)}
    got["z1"], got["z3"] = z_move(own, 1), z_move(own, 3)
    weight = after(gate_up_w, own).transpose(2, 0, 1, 3)
    got["x0_c"] = core_move(got["x0"])
    got["x1"], got["z1_c"] = x_move(got["z1"]), core_move(got["z1"])
    got["z2"] = z_move(got["z1"], 1)
    groups = (("own", "x0"), ("z1", "x1"), ("z2", "x2"), ("z3", "x3"))
    t = [own]

    def up(g):
        near, far = groups[g]
        blocks = [got[k] for k in (near, far, near + "_c", far + "_c")]
        t[:] = [up_step(g, blocks, *t)]

    def act(g):
        t[:] = [act_step(g, *t)]

    def lower(g):
        t[:] = [down_step(g, *t)]

    def gather(g):
        t[:] = [sum_step(g, False, *t)]
        moving["x", g] = x_move(t[0])

    def total(g):
        whole = add(after(mine, *t), sums[g][:1], [moving["x", g]], False)
        t[:] = whole
        moving["z", g] = z_move(whole[0], (0, 3, 2, 1)[g])

    def across(g):
        got["x%d" % g] = x_move(after(got["z%d" % g], *t))

    def b_free(g):
        got["x%d_c" % g] = core_move(got["x%d" % g])

    def across_next(g):
        got["x%d" % g] = x_move(after(got["z%d" % g], got["x%d" % (g - 1)]))

    def near_core(g):
        got["z%d_c" % g] = core_move(after(got["z%d" % g], *t))

    def far_core(g):
        got["x%d_c" % g] = core_move(after(got["x%d" % g], *t))

    def tables(g):
        kv_w = turn(after(mine, *t), kv_proj)
        pages, position = page_list(
            after(mine, kv_w), kv_cache.shape[0], prompt_lens, decode_pos, table
        )
        lane = jnp.arange(columns, dtype=jnp.int32)
        inverse = jnp.exp(
            -((lane % (HD // 2)).astype(F32) * (2.0 / HD)) * jnp.log(F32(ROPE_BASE))
        )
        angles = position[:, :1] * inverse[None, :]
        is_key = (my_col * columns + lane < KVH * HD)[None, :]
        cosine = jnp.where(is_key, jnp.cos(angles), 1.0)
        sine = jnp.where(is_key, jnp.sin(angles), 0.0)
        got["tables"] = lax.optimization_barrier((kv_w, pages, cosine, sine))
        t.append(got["tables"][2])

    def cache_copy(g):
        got["cache"] = copy_cache(after(kv_cache, *t))
        t.append(got["cache"])

    def arrived(g):
        t.append(got["z%d" % g])

    def back(g):
        t.append(moving["x", g])

    def home(g):
        t.append(moving["z", g])

    steps = dict(U=up, A=act, D=lower, S=gather, T=total, X=across, N=across_next, Q=near_core, B=far_core)
    steps.update(b=b_free, K=tables, C=cache_copy, W=arrived, V=back, H=home)
    for name, g in ORDER:
        steps[name](g)
    kv_w, pages, cosine, sine = got["tables"]
    cache = got["cache"]
    whole = lambda a, b: a.astype(F32) + b.astype(F32)
    mixture = whole(sums[0][0], moving["x", 0]) + whole(moving["z", 1], moving["z", 3])
    mixture = mixture + moving["z", 2].astype(F32)
    layer_out = lax.optimization_barrier((res_f + mixture).astype(BF))

    rotated = keys_values(
        layer_out, y_move(layer_out), gain_moe, gain_other, kv_w, cosine, sine
    )

    x0 = x_move(rotated)
    z1 = z_move(rotated, 1)
    z3 = z_move(rotated, 3)
    x1 = x_move(after(z1, x0))
    z2 = z_move(z1, 1)
    x3 = x_move(z3)
    x2 = x_move(after(z2, x1))
    kv_blocks = []
    for together in ((rotated, x0), (z1, z3, x1), (z2, x3), (x2,)):
        block = stack(*together) if len(together) > 1 else together[0]
        kv_blocks += [block, core_move(block)]
    written = write_pages(pages, kv_blocks, cache)
    return (layer_out, written)


def solution(mesh):
    body = on_device_16x2 if (mesh.shape["dp"], mesh.shape["mp"]) == (NZ * NX * NC, 2) else on_device
    placed = (
        P("dp", "mp"),
        P("dp", "mp"),
        P(None, "mp"),
        P("mp"),
        P("dp", None),
        P("dp", None),
        P("dp", "mp", None, None),
        P("dp", None, "mp"),
        P("mp"),
        P(None, "mp"),
        P(),
        P(),
        P(),
        P("dp", None, "mp"),
    )
    return jax.shard_map(
        body,
        mesh=mesh,
        in_specs=placed,
        out_specs=(P("dp", "mp"), P("dp", None, "mp")),
        check_vma=False,
    )
```
